256 devices in a mesh: row: 16 (over y_hi, z), col: 8 (over x, core), rhs: 2 (over y_lo).
Axes of the slice: x: 4, y: 4 (y_hi: 2, y_lo: 2; y = y_hi * 2 + y_lo), z: 8, core: 2. Of those that a mesh axis runs over, the one named last changes fastest.
Arguments:
- lower: float32 [6, 2048, 4, 2048], P(None, 'row', None, 'col'), may hold values from -0.0625 to 0.0625
- inverse: float32 [4, 2048, 2048], P(None, ('col', 'rhs'), 'row'), may hold values from -0.125 to 0.125
- right_side: float32 [6, 2048, 2048], P(None, 'row', 'rhs'), may hold values from -6 to 6
Outputs:
- solved: float32 [4, 2048, 2048], P(None, 'col', 'rhs')
- trailing: float32 [2, 2048, 2048], P(None, 'row', 'rhs')
The draws below stay inside these ranges and needn't reach their ends.
All inputs are finite; a program needn't handle non-finite values.
Results may differ from the reference program's by a relative error of at most 0.0001.
Values sent between devices are 32-bit elements; how exact they have to be, the bound alone decides.
No kernel may reach another device: no remote copies, remote signals or barrier semaphores. Data moves between devices by JAX's collectives and lax.ppermute only.
A program may use at most 64 MiB of HBM per device.

```python
import jax
import jax.numpy as jnp
from jax import lax

NB = 2048
NRHS = 2048
KB = 4
BLOCKS = 6


def block_levels(own_key, dims, pieces, least, largest):
    loudness, own = 1.0, jax.random.fold_in(own_key, 6)
    for axis_at, parts in pieces:
        draws = jnp.exp(jax.random.uniform(jax.random.fold_in(own, axis_at), (parts,), jnp.float32, least / len(pieces), largest / len(pieces)))
        loudness = loudness * jnp.repeat(draws, dims[axis_at] // parts).reshape([-1 if axis == axis_at else 1 for axis in range(len(dims))])
    return loudness


def bell_draw(rng, dims, scale, bound, shards=(), dtype=jnp.bfloat16):
    entries = jax.random.normal(rng, dims, jnp.float32) * scale
    if len(shards) > 0:
        entries = block_levels(rng, dims, shards, -0.22, 0.18) * entries
    return jnp.clip(entries, min=-bound, max=bound).astype(dtype)


def setup_inputs(seed: int = 0) -> dict:
    key_list = jax.random.split(jax.random.key(seed), 4)
    lower = bell_draw(key_list[0], (BLOCKS, NB, KB, NB), (KB * NB) ** -0.5, 0.0625, ((1, 16), (3, 8)), jnp.float32)
    inverse = bell_draw(key_list[1], (KB, NB, NB), NB ** -0.5, 0.125, ((1, 16), (2, 16)), jnp.float32)
    right_side = bell_draw(key_list[2], (BLOCKS, NB, NRHS), 1.0, 6.0, ((1, 16), (2, 2)), jnp.float32)
    return dict(lower=lower, inverse=inverse, right_side=right_side)


def reference(lower, inverse, right_side):
    accum = jnp.zeros_like(right_side)
    solved_list = []
    for k in range(KB):
        residual_block = right_side[k] - accum[k]
        unknowns = jnp.dot(inverse[k], residual_block, precision=lax.Precision.HIGHEST, preferred_element_type=jnp.float32)
        solved_list.append(unknowns)
        update = jnp.einsum("inc,cr->inr", lower[k + 1:, :, k, :], unknowns, precision=lax.Precision.HIGHEST)
        accum = jnp.concatenate([accum[:k + 1], accum[k + 1:] + update], axis=0)
    return jnp.stack(solved_list), right_side[KB:] - accum[KB:]
```

```python
import jax
import jax.numpy as jnp
from jax import lax
from jax.sharding import Mesh
from jax.sharding import PartitionSpec as P


AXES = ("yh", "z", "x", "core", "yl")
SIZES = (2, 8, 4, 2, 2)


def dot(a, b):
    return jnp.dot(a, b, precision=lax.Precision.HIGHEST, preferred_element_type=jnp.float32)


def swap(value, axis):
    return lax.ppermute(value, axis, [(0, 1), (1, 0)])


def natural(mine, other, axis, dim):
    at = lax.axis_index(axis)
    return jnp.where(
        at == 0, jnp.concatenate([mine, other], dim), jnp.concatenate([other, mine], dim)
    )


def reduce_rows(partial, axis):
    n = lax.axis_size(axis)
    pieces = partial.reshape(n, partial.shape[0] // n, partial.shape[1])
    return jnp.sum(lax.all_to_all(pieces, axis, 0, 0), axis=0)


def gather_rows(value, axis):
    n = lax.axis_size(axis)
    copies = jnp.broadcast_to(value[None], (n, *value.shape))
    return lax.all_to_all(copies, axis, 0, 0).reshape(n * value.shape[0], value.shape[1])


def on_device(lower, inverse, right_side):
    chain, blocks = inverse.shape[0], right_side.shape[0]
    rows, width = right_side.shape[1:]
    yh, core = lax.axis_index("yh"), lax.axis_index("core")
    part = width // 4

    def inverse_of(k):
        mine = inverse[k]
        mine = jnp.concatenate([mine, swap(mine, "yh")], 1)
        mine = natural(mine, swap(mine, "yl"), "yl", 0)
        return jnp.concatenate([mine, swap(mine, "core")], 0)

    def right_of(k):
        mine = lax.dynamic_slice_in_dim(right_side[k], (yh * 2 + core) * part, part, 1)
        send = lax.dynamic_slice_in_dim(right_side[k], ((1 - yh) * 2 + core) * part, part, 1)
        return jnp.concatenate([mine, swap(send, "yh")], 0)

    def lower_of(i):
        many = min(i, chain)
        mine = jnp.stack([lower[i, :, j, :] for j in range(many)])
        mine = jnp.concatenate([mine, swap(mine, "yh")], 1)
        return jnp.concatenate([mine, swap(mine, "core")], 2)

    inverses = [inverse_of(k) for k in range(chain)]
    rights = [right_of(k) for k in range(chain)]
    lowers = [None] + [lower_of(i) for i in range(1, blocks)]

    solved, placed = [], []
    residual = rights[0]
    for k in range(chain):
        piece = reduce_rows(dot(inverses[k], residual), "z")
        unknowns = gather_rows(piece, "z")
        solved.append(unknowns)
        half = unknowns.shape[0] // 2
        columns = natural(unknowns[:half], swap(unknowns[half:], "core"), "core", 1)
        placed.append(natural(columns, swap(columns, "yh"), "yh", 1))
        if k + 1 < chain:
            update = sum(dot(lowers[k + 1][j], solved[j]) for j in range(k + 1))
            update = gather_rows(reduce_rows(update, "x"), "x")
            residual = rights[k + 1] - update

    tail = jnp.stack(
        [sum(dot(lowers[i][j], solved[j]) for j in range(chain)) for i in range(chain, blocks)]
    )
    n = lax.axis_size("x")
    count = blocks - chain
    tail = tail.reshape(count, 2, n, rows // n, part).transpose(2, 0, 1, 3, 4)
    tail = jnp.sum(lax.all_to_all(tail, "x", 0, 0), axis=0)
    tail = natural(tail[:, 0], swap(tail[:, 1], "yh"), "yh", 2)
    tail = jnp.broadcast_to(tail[None], (n, *tail.shape))
    tail = lax.all_to_all(tail, "x", 0, 0).transpose(1, 0, 2, 3).reshape(count, rows, 2 * part)
    other = swap(tail, "core")
    first = jnp.where(core == 0, tail, other)
    second = jnp.where(core == 0, other, tail)
    tail = jnp.concatenate(
        [first[..., :part], second[..., :part], first[..., part:], second[..., part:]], 2
    )
    return jnp.stack(placed), right_side[chain:] - tail


def solution(mesh):
    fine = Mesh(mesh.devices.reshape(SIZES), AXES)
    return jax.shard_map(
        on_device,
        mesh=fine,
        in_specs=(
            P(None, ("yh", "z"), None, ("x", "core")),
            P(None, ("x", "core", "yl"), ("yh", "z")),
            P(None, ("yh", "z"), "yl"),
        ),
        out_specs=(P(None, ("x", "core"), "yl"), P(None, ("yh", "z"), "yl")),
        check_vma=False,
    )
```

```python
import jax
import jax.numpy as jnp
from jax import lax
from jax.experimental import pallas as pl
from jax.experimental.pallas import tpu as pltpu
from jax.sharding import Mesh
from jax.sharding import PartitionSpec as P


AXES = ("yh", "z", "x", "core", "yl")
SIZES = (2, 8, 4, 2, 2)
F32 = jnp.float32
SMEM = pl.BlockSpec(memory_space=pltpu.SMEM)


def dot(a, b):
    return jnp.dot(a, b, precision=lax.Precision.HIGHEST, preferred_element_type=F32)


def whole(array):
    return pl.BlockSpec(array.shape, lambda _: (0,) * len(array.shape), pipeline_mode=pl.Buffered(1))


def call(kernel, out_shape, scalars, arrays, scratch=(), flops=0):
    size = sum(a.size * 4 for a in arrays)
    many = isinstance(out_shape, list)
    return pl.pallas_call(
        kernel,
        grid=(1,),
        out_shape=out_shape,
        in_specs=[SMEM] * len(scalars) + [whole(a) for a in arrays],
        out_specs=[whole(o) for o in out_shape] if many else whole(out_shape),
        scratch_shapes=list(scratch),
        compiler_params=pltpu.CompilerParams(vmem_limit_bytes=60 << 20),
        cost_estimate=pl.CostEstimate(flops=flops, bytes_accessed=2 * size, transcendentals=0),
    )(*scalars, *arrays)


def swap(value, axis):
    return lax.ppermute(value, axis, [(0, 1), (1, 0)])


def ring(value, axis, by):
    n = lax.axis_size(axis)
    return lax.ppermute(value, axis, [(i, (i + by) % n) for i in range(n)])


def hold(first, *others):
    return lax.optimization_barrier((first, *others))


def take_blocks(lower, groups):
    rows, columns = lower.shape[1], lower.shape[3]

    def kernel(lower_ref, *outs):
        for out, group in zip(outs, groups):
            for at, (i, j) in enumerate(group):
                out[at * rows : (at + 1) * rows, :] = lower_ref[i, :, j, :]

    shapes = [jax.ShapeDtypeStruct((len(g) * rows, columns), F32) for g in groups]
    return call(kernel, shapes, [], [lower])


def solve_part(k, own_half, pieces, right, partials):
    m = right[0].shape[0] // right[2]
    n = pieces[0].shape[1]
    at = k[0]
    width = right[0].shape[1]

    def kernel(half_ref, *refs):
        pieces_ref, (b0, b1), parts = refs[:8], refs[8:10], refs[10 : 10 + len(partials)]
        out, inv, res = refs[10 + len(partials) :]
        half = half_ref[0]
        for c in range(2):
            for y in range(2):
                off = pl.multiple_of((half if y == 0 else 1 - half) * n + c * 2 * n, n)
                for h in range(2):
                    inv[pl.ds(off, n), h * n : (h + 1) * n] = pieces_ref[c * 4 + y * 2 + h][
                        at * n : (at + 1) * n, :
                    ]
        for h, b in enumerate((b0, b1)):
            value = b[k[1] * m : (k[1] + 1) * m, :]
            if parts:
                total = parts[0][h * m : (h + 1) * m, :]
                for p in parts[1:]:
                    total = total + p[h * m : (h + 1) * m, :]
                value = value - total
            res[h * m : (h + 1) * m, :] = value

        @pl.loop(0, 4)
        def _(t):
            here = pl.ds(pl.multiple_of(t * n, n), n)
            out[here, :] = dot(inv[here, :], res[...])

    return call(
        kernel,
        jax.ShapeDtypeStruct((4 * n, width), F32),
        [own_half],
        [*pieces, *right[:2], *partials],
        [pltpu.VMEM((4 * n, 2 * n), F32), pltpu.VMEM((2 * m, width), F32)],
        flops=2 * 4 * n * 2 * n * width,
    )


def update_part(groups, ats, solved, before=None):
    rows = groups[0].shape[0] // ats[0]
    columns = groups[0].shape[1]
    width = solved[0].shape[1]
    picks = ats[1]
    outer = len(picks)

    def kernel(*refs):
        g, s = refs[:4], refs[4 : 4 + len(solved)]
        out = refs[-1]
        for o, pick in enumerate(picks):
            for h in range(2):
                place = slice((o * 2 + h) * rows, (o * 2 + h + 1) * rows)
                total = None if before is None else refs[4 + len(solved)][place, :]
                for at, s_ref in zip(pick, s):
                    for c in range(2):
                        left = g[h + 2 * c][at * rows : (at + 1) * rows, :]
                        term = dot(left, s_ref[c * columns : (c + 1) * columns, :])
                        total = term if total is None else total + term
                out[place, :] = total

    return call(
        kernel,
        jax.ShapeDtypeStruct((outer * 2 * rows, width), F32),
        [],
        [*groups, *solved, *([] if before is None else [before])],
        flops=2 * outer * 2 * rows * 2 * columns * len(solved) * width,
    )


def sum_copies(pieces):
    def kernel(in_ref, out_ref):
        n = in_ref.shape[0]
        total = in_ref[0]
        for i in range(1, n):
            total = total + in_ref[i]
        for i in range(n):
            out_ref[i] = total

    return call(kernel, jax.ShapeDtypeStruct(pieces.shape, F32), [], [pieces])


def on_device(lower, inverse, right_side):
    chain, blocks = inverse.shape[0], right_side.shape[0]
    rows, width = right_side.shape[1:]
    part = width // 4
    yh, z, x, core, yl = (lax.axis_index(a) for a in AXES)
    nz, nx = lax.axis_size("z"), lax.axis_size("x")
    half = yl.astype(jnp.int32).reshape(1)

    def spread(value):
        across = [
            value,
            swap(value, "yh"),
            swap(value, "yl"),
            lax.ppermute(value, ("yh", "yl"), [(i, 3 - i) for i in range(4)]),
        ]
        return across + [swap(v, "core") for v in across]

    def right_of(first, last):
        size = (last - first, rows, part)
        mine = lax.dynamic_slice(right_side, (first, 0, (yh * 2 + core) * part), size)
        send = lax.dynamic_slice(right_side, (first, 0, ((1 - yh) * 2 + core) * part), size)
        mine, send = (v.reshape(-1, part) for v in (mine, send))
        return mine, swap(send, "yh"), last - first

    def spread_lower(value):
        other = swap(value, "yh")
        return [value, other, swap(value, "core"), swap(other, "core")]

    flat = inverse.reshape(-1, inverse.shape[2])
    first_inverse = spread(flat[:rows])
    first_right = right_of(0, 1)
    rest_inverse = spread(flat[rows:])
    rest_right = right_of(1, chain)

    group_of = [[(1, 0)], [(2, 0), (2, 1), (3, 0), (3, 1), (3, 2)]]
    group_of.append([(i, j) for i in range(chain, blocks) for j in range(chain)])
    taken = take_blocks(lower, group_of)
    near, mid, far = (spread_lower(v) for v in taken)
    tails = [[i * chain + j for j in range(chain)] for i in range(blocks - chain)]

    def z_sum(value):
        return lax.all_to_all(value.reshape(nz, -1, part), "z", 0, 0)

    def z_all(value):
        return lax.all_to_all(sum_copies(value), "z", 0, 0).reshape(-1, part)

    def x_all(value):
        return [value] + [ring(value, "x", by) for by in range(1, nx)]

    def quarters(unknowns):
        size = unknowns.shape[0] // 2
        a = unknowns[:size]
        b = swap(unknowns[size:], "core")
        return [a, b, swap(a, "yh"), swap(b, "yh")]

    def place(out, k, four):
        for at, value in enumerate(four):
            p = yh if at < 2 else 1 - yh
            q = core if at % 2 == 0 else 1 - core
            out = lax.dynamic_update_slice(out, value[None], (k, 0, (p * 2 + q) * part))
        return out

    out = jnp.zeros((chain, lower.shape[3], width), F32)

    summed = z_sum(solve_part((0, 0), half, first_inverse, first_right, []))
    summed, *near = hold(summed, *near)
    s0 = z_all(summed)
    s0, *rest = hold(s0, *rest_inverse, rest_right[0], rest_right[1])
    rest_inverse, rest_right = rest[:-2], (*rest[-2:], rest_right[2])

    parts = x_all(update_part(near, (1, [[0]]), [s0]))
    summed = z_sum(solve_part((0, 0), half, rest_inverse, rest_right, parts))
    ahead = update_part(mid, (5, [[0], [2]]), [s0])
    summed, ahead = hold(summed, ahead)
    s1 = z_all(summed)
    four = quarters(s0)
    s1, *four = hold(s1, *four)
    out = place(out, 0, four)

    parts = x_all(update_part(mid, (5, [[1]]), [s1], ahead[: 2 * rows]))
    summed = z_sum(solve_part((1, 1), half, rest_inverse, rest_right, parts))
    ahead = update_part(mid, (5, [[3]]), [s1], ahead[2 * rows :])
    summed, ahead, out = hold(summed, ahead, out)
    s2 = z_all(summed)
    four = quarters(s1)
    s2, *four = hold(s2, *four)
    out = place(out, 1, four)

    parts = x_all(update_part(mid, (5, [[4]]), [s2], ahead))
    summed = z_sum(solve_part((2, 2), half, rest_inverse, rest_right, parts))
    last = update_part(far, (len(group_of[2]), [t[:2] for t in tails]), [s0, s1])
    four = quarters(s2)
    summed, last, out = hold(summed, last, out)
    s3 = z_all(summed)
    last = update_part(far, (len(group_of[2]), [t[2:3] for t in tails]), [s2], last)
    s3, last, *four = hold(s3, last, *four)
    out = place(out, 2, four)

    last = update_part(far, (len(group_of[2]), [t[3:] for t in tails]), [s3], last)
    four = quarters(s3)
    n, count = rows // nx, blocks - chain
    pieces = last.reshape(count, 2, nx, n, part)
    own = lax.dynamic_index_in_dim(pieces, x, 2, keepdims=False)
    for by in range(1, nx):
        own = own + ring(lax.dynamic_index_in_dim(pieces, (x + by) % nx, 2, keepdims=False), "x", by)
    own = jnp.stack([own[:, 0], swap(own[:, 1], "yh")])
    tail = jnp.zeros((count, rows, width), F32)
    for by in range(nx):
        value = own if by == 0 else ring(own, "x", by)
        for c in range(2):
            here = value if c == 0 else swap(value, "core")
            q = core if c == 0 else 1 - core
            for h in range(2):
                p = yh if h == 0 else 1 - yh
                tail = lax.dynamic_update_slice(
                    tail, here[h], (0, ((x - by) % nx) * n, (p * 2 + q) * part)
                )
    out = place(out, 3, four)
    return out, right_side[chain:] - tail


def solution(mesh):
    fine = Mesh(mesh.devices.reshape(SIZES), AXES)
    return jax.shard_map(
        on_device,
        mesh=fine,
        in_specs=(
            P(None, ("yh", "z"), None, ("x", "core")),
            P(None, ("x", "core", "yl"), ("yh", "z")),
            P(None, ("yh", "z"), "yl"),
        ),
        out_specs=(P(None, ("x", "core"), "yl"), P(None, ("yh", "z"), "yl")),
        check_vma=False,
    )
```

```python
import jax
import jax.numpy as jnp
from jax import lax
from jax.experimental import pallas as pl
from jax.experimental.pallas import tpu as pltpu
from jax.sharding import Mesh
from jax.sharding import PartitionSpec as P

LIMIT = 60 << 20

AXES = ("yh", "z", "x", "core", "yl")
SIZES = (2, 8, 4, 2, 2)
F32 = jnp.float32
SMEM = pl.BlockSpec(memory_space=pltpu.SMEM)


def dot(a, b):
    return jnp.dot(a, b, precision=lax.Precision.HIGHEST, preferred_element_type=F32)


def block(shape, *at):
    return pl.BlockSpec(shape, lambda _: at, pipeline_mode=pl.Buffered(1))


def whole(array):
    return block(array.shape, *(0,) * len(array.shape))


def call(kernel, out_shape, scalars, arrays, scratch=(), flops=0, out_specs=None, alias=None):
    pairs = [a if isinstance(a, tuple) else (a, whole(a)) for a in arrays]
    pairs = [(p[0], block(p[1], *p[2])) if len(p) == 3 else p for p in pairs]
    many = isinstance(out_shape, list)
    if out_specs is None:
        out_specs = [whole(o) for o in out_shape] if many else whole(out_shape)
    outs = sum(4 * o.size for o in (out_shape if many else [out_shape]))
    return pl.pallas_call(
        kernel,
        grid=(1,),
        out_shape=out_shape,
        in_specs=[SMEM] * len(scalars) + [spec for _, spec in pairs],
        out_specs=out_specs,
        scratch_shapes=list(scratch),
        input_output_aliases=alias or {},
        compiler_params=pltpu.CompilerParams(vmem_limit_bytes=LIMIT),
        cost_estimate=pl.CostEstimate(flops=flops, bytes_accessed=2 * outs, transcendentals=0),
    )(*scalars, *(array for array, _ in pairs))


def swap(value, axis):
    return lax.ppermute(value, axis, [(0, 1), (1, 0)])


def ring(value, axis, by):
    n = lax.axis_size(axis)
    return lax.ppermute(value, axis, [(i, (i + by) % n) for i in range(n)])


def hold(first, *others):
    return lax.optimization_barrier((first, *others))


def take_blocks(lower, groups):
    rows, columns = lower.shape[1], lower.shape[3]

    def kernel(lower_ref, *outs):
        for out, group in zip(outs, groups):
            for at, (i, j) in enumerate(group):
                out[at * rows : (at + 1) * rows, :] = lower_ref[i, :, j, :]

    shapes = [jax.ShapeDtypeStruct((len(g) * rows, columns), F32) for g in groups]
    return call(kernel, shapes, [], [lower])


def solve_part(half, inverse, k, right, at, partials):
    m, n = right[0].shape[0] // right[2], inverse[0].shape[1]
    width = right[0].shape[1]

    def kernel(half_ref, *refs):
        pieces, (b0, b1), parts = refs[:8], refs[8:10], refs[10 : 10 + len(partials)]
        out, inv, res = refs[10 + len(partials) :]
        for c in range(2):
            for y in range(2):
                off = half_ref[0] if y == 0 else 1 - half_ref[0]
                off = pl.multiple_of(off * n + c * 2 * n, n)
                for h in range(2):
                    inv[pl.ds(off, n), h * n : (h + 1) * n] = pieces[c * 4 + y * 2 + h][...]
        for h, b in enumerate((b0, b1)):
            value = b[...]
            for p in parts:
                total = p[0, h * m : (h + 1) * m, :]
                for i in range(1, p.shape[0]):
                    total = total + p[i, h * m : (h + 1) * m, :]
                value = value - total
            res[h * m : (h + 1) * m, :] = value

        @pl.loop(0, 4)
        def _(t):
            here = pl.ds(pl.multiple_of(t * n, n), n)
            out[here, :] = dot(inv[here, :], res[...])

    return call(
        kernel,
        jax.ShapeDtypeStruct((4 * n, width), F32),
        [half],
        [(p, (n, n), (k, 0)) for p in inverse]
        + [(b, (m, width), (at, 0)) for b in right[:2]]
        + list(partials),
        [pltpu.VMEM((4 * n, 2 * n), F32), pltpu.VMEM((2 * m, width), F32)],
        flops=2 * 4 * n * 2 * n * width,
    )


def lower_blocks(group, picks, rows):
    return [(g, (rows, g.shape[1]), (at, 0)) for pick in picks for at in pick for g in group]


def stack_products(refs, outer, rows, solved, left, right):
    columns = refs[0].shape[1]
    many = len(solved)
    for o in range(outer):
        for j in range(many):
            for h in range(2):
                for c in range(2):
                    at = (o * many + j) * 4 + h + 2 * c
                    left[o * 2 + h, j * 2 + c] = refs[at][...]
    for j, s in enumerate(solved):
        for c in range(2):
            right[j * 2 + c] = s[c * columns : (c + 1) * columns, :]

    def product(t):
        total = dot(left[t, 0], right[0])
        for i in range(1, 2 * many):
            total = total + dot(left[t, i], right[i])
        return total

    return product


def product_scratch(outer, rows, columns, many, width):
    return [
        pltpu.VMEM((outer * 2, many * 2, rows, columns), F32),
        pltpu.VMEM((many * 2, columns, width), F32),
    ]


def update_part(group, picks, solved, rows, copies=0):
    width, columns, outer = solved[0].shape[1], group[0].shape[1], len(picks)
    blocks = lower_blocks(group, picks, rows)

    def kernel(*refs):
        out, left, right = refs[-3:]
        product = stack_products(refs, outer, rows, refs[len(blocks) : -3], left, right)

        @pl.loop(0, outer * 2)
        def _(t):
            here = pl.ds(pl.multiple_of(t * rows, rows), rows)
            value = product(t)
            if copies:
                for i in range(copies):
                    out[i, here, :] = value
            else:
                out[here, :] = value

    size = (outer * 2 * rows, width)
    return call(
        kernel,
        jax.ShapeDtypeStruct((copies, *size) if copies else size, F32),
        [],
        blocks + list(solved),
        product_scratch(outer, rows, columns, len(solved), width),
        flops=2 * len(blocks) * rows * columns * width,
    )


def tail_part(x, group, picks, solved, before, rows, n):
    width, columns = solved.shape[1], group[0].shape[1]
    blocks = lower_blocks(group, picks, rows)
    count, share = len(picks), rows // n

    def kernel(x_ref, *refs):
        s, b = refs[len(blocks)], refs[len(blocks) + 1]
        outs, (total, left, right) = refs[len(blocks) + 2 : -3], refs[-3:]
        product = stack_products(refs, count, rows, [s], left, right)

        @pl.loop(0, count * 2)
        def _(t):
            here = pl.ds(pl.multiple_of(t * rows, rows), rows)
            total[t] = b[here, :] + product(t)

        for d in range(n):
            off = pl.multiple_of(lax.rem(x_ref[0] + d, n) * share, share)
            for t in range(count * 2):
                outs[d][t // 2, t % 2] = total[t, pl.ds(off, share), :]

    return call(
        kernel,
        [jax.ShapeDtypeStruct((count, 2, share, width), F32)] * n,
        [x],
        [*blocks, solved, before],
        [pltpu.VMEM((count * 2, rows, width), F32)]
        + product_scratch(count, rows, columns, 1, width),
        flops=2 * len(blocks) * rows * columns * width,
    )


def sum_copies(pieces):
    def kernel(in_ref, out_ref):
        n = in_ref.shape[0]
        total = in_ref[0]
        for i in range(1, n):
            total = total + in_ref[i]
        for i in range(n):
            out_ref[i] = total

    return call(kernel, jax.ShapeDtypeStruct(pieces.shape, F32), [], [pieces])


def place(yh, core, out, first, four, shape):
    rows, size = shape[1], four[0].shape[1]
    many = four[0].shape[0] // rows

    def kernel(yh_ref, core_ref, *refs):
        for at in range(4):
            p = yh_ref[0] if at < 2 else 1 - yh_ref[0]
            q = core_ref[0] if at % 2 == 0 else 1 - core_ref[0]
            off = pl.multiple_of((p * 2 + q) * size, size)
            for k in range(many):
                refs[-1][k, :, pl.ds(off, size)] = refs[at][k * rows : (k + 1) * rows, :]

    old = [] if out is None else [(out, pl.BlockSpec(memory_space=pl.ANY))]
    return call(
        kernel,
        jax.ShapeDtypeStruct(shape, F32),
        [yh, core],
        list(four) + old,
        out_specs=block((many, *shape[1:]), first // many, 0, 0),
        alias=None if out is None else {6: 0},
    )


def finish(yh, core, pieces, right_side, first):
    _, rows, width = right_side.shape
    n, count, _, share, size = pieces[0].shape

    def kernel(yh_ref, core_ref, right_ref, *refs):
        for h in range(2):
            for c in range(2):
                p = yh_ref[0] if h == 0 else 1 - yh_ref[0]
                q = core_ref[0] if c == 0 else 1 - core_ref[0]
                lanes = pl.ds(pl.multiple_of((p * 2 + q) * size, size), size)
                for d in range(n):
                    here = slice(d * share, (d + 1) * share)
                    refs[-1][:, here, lanes] = right_ref[:, here, lanes] - refs[c][d, :, h]

    return call(
        kernel,
        jax.ShapeDtypeStruct((count, rows, width), F32),
        [yh, core],
        [(right_side, (count, rows, width), (first // count, 0, 0)), *pieces],
    )


def on_device(lower, inverse, right_side):
    chain, blocks = inverse.shape[0], right_side.shape[0]
    rows, width = right_side.shape[1:]
    part = width // 4
    yh, z, x, core, yl = (lax.axis_index(a).astype(jnp.int32) for a in AXES)
    nz, nx = lax.axis_size("z"), lax.axis_size("x")
    half, yh1, x1, core1 = (v.reshape(1) for v in (yl, yh, x, core))

    def spread(value):
        four = [
            value,
            swap(value, "yh"),
            swap(value, "yl"),
            lax.ppermute(value, ("yh", "yl"), [(i, 3 - i) for i in range(4)]),
        ]
        return four + [swap(v, "core") for v in four]

    def right_of(first, last):
        size = (last - first, rows, part)
        mine = lax.dynamic_slice(right_side, (first, 0, (yh * 2 + core) * part), size)
        send = lax.dynamic_slice(right_side, (first, 0, ((1 - yh) * 2 + core) * part), size)
        mine, send = (v.reshape(-1, part) for v in (mine, send))
        return mine, swap(send, "yh"), last - first

    def spread_lower(value):
        other = swap(value, "yh")
        return [value, other, swap(value, "core"), swap(other, "core")]

    flat = inverse.reshape(-1, inverse.shape[2])
    first_inverse = spread(flat[:rows])
    first_right = right_of(0, 1)
    rest_inverse = spread(flat[rows:])
    rest_right = right_of(1, chain)

    group_of = [[(1, 0), (2, 0), (2, 1), (3, 0), (3, 1), (3, 2)]]
    group_of.append([(i, j) for i in range(chain, blocks) for j in range(chain)])
    near, far = (spread_lower(v) for v in take_blocks(lower, group_of))
    tails = [[i * chain + j for j in range(chain)] for i in range(blocks - chain)]

    def z_sum(value):
        return lax.all_to_all(value.reshape(nz, -1, part), "z", 0, 0)

    def z_all(value):
        return lax.all_to_all(sum_copies(value), "z", 0, 0).reshape(-1, part)

    def step(k, solved):
        picks = [[k * (k - 1) // 2 + j for j in range(k)]]
        return [lax.all_to_all(update_part(near, picks, solved, rows, nx), "x", 0, 0)]

    def quarters(many):
        size = many[0].shape[0] // 2
        a, b = (jnp.concatenate(v, 0) if len(many) > 1 else v[0] for v in (
            [s[:size] for s in many], [s[size:] for s in many]))
        b = swap(b, "core")
        return [a, b, swap(a, "yh"), swap(b, "yh")]

    shape = (chain, lower.shape[3], width)

    summed = z_sum(solve_part(half, first_inverse, 0, first_right, 0, []))
    s0 = z_all(summed)
    s0, *near = hold(s0, *near)

    parts = step(1, [s0])
    parts[0], *rest = hold(parts[0], *rest_inverse, rest_right[0], rest_right[1])
    rest_inverse, rest_right = rest[:-2], (*rest[-2:], rest_right[2])
    s1 = z_all(z_sum(solve_part(half, rest_inverse, 0, rest_right, 0, parts)))

    parts = step(2, [s0, s1])
    s2 = z_all(z_sum(solve_part(half, rest_inverse, 1, rest_right, 1, parts)))

    parts = step(3, [s0, s1, s2])
    parts[0], *far = hold(parts[0], *far)
    summed = z_sum(solve_part(half, rest_inverse, 2, rest_right, 2, parts))
    before = update_part(far, [t[:3] for t in tails], [s0, s1, s2], rows)
    four = quarters([s0, s1, s2])
    summed, before = hold(summed, before)
    s3 = z_all(summed)
    s3, *four = hold(s3, *four)

    pieces = tail_part(x1, far, [t[3:] for t in tails], s3, before, rows, nx)
    last = quarters([s3])
    out = place(yh1, core1, None, 0, four, shape)
    own = pieces[0]
    for by in range(1, nx):
        own = own + ring(pieces[by], "x", by)
    own = jnp.stack([own[:, 0], swap(own[:, 1], "yh")], 1)
    own, out = hold(own, out)
    final = lax.all_to_all(jnp.broadcast_to(own[None], (nx, *own.shape)), "x", 0, 0)
    final = [final, swap(final, "core")]
    out = place(yh1, core1, out, 3, last, shape)
    return out, finish(yh1, core1, final, right_side, chain)


def solution(mesh):
    fine = Mesh(mesh.devices.reshape(SIZES), AXES)
    return jax.shard_map(
        on_device,
        mesh=fine,
        in_specs=(
            P(None, ("yh", "z"), None, ("x", "core")),
            P(None, ("x", "core", "yl"), ("yh", "z")),
            P(None, ("yh", "z"), "yl"),
        ),
        out_specs=(P(None, ("x", "core"), "yl"), P(None, ("yh", "z"), "yl")),
        check_vma=False,
    )
```

```python
import jax
import jax.numpy as jnp
from jax import lax
from jax.experimental import pallas as pl
from jax.experimental.pallas import tpu as pltpu
from jax.sharding import Mesh
from jax.sharding import PartitionSpec as P

LIMIT = 60 << 20

AXES = ("yh", "z", "x", "core", "yl")
SIZES = (2, 8, 4, 2, 2)
F32 = jnp.float32
SMEM = pl.BlockSpec(memory_space=pltpu.SMEM)


def dot(a, b):
    return jnp.dot(a, b, precision=lax.Precision.HIGHEST, preferred_element_type=F32)


def block(shape, *at):
    return pl.BlockSpec(shape, lambda _: at, pipeline_mode=pl.Buffered(1))


def whole(array):
    return block(array.shape, *(0,) * len(array.shape))


def call(
    kernel, out_shape, scalars, arrays, scratch=(), flops=0, out_specs=None, alias=None, limit=LIMIT
):
    pairs = [a if isinstance(a, tuple) else (a, whole(a)) for a in arrays]
    pairs = [(p[0], block(p[1], *p[2])) if len(p) == 3 else p for p in pairs]
    many = isinstance(out_shape, list)
    if out_specs is None:
        out_specs = [whole(o) for o in out_shape] if many else whole(out_shape)
    outs = sum(4 * o.size for o in (out_shape if many else [out_shape]))
    return pl.pallas_call(
        kernel,
        grid=(1,),
        out_shape=out_shape,
        in_specs=[SMEM] * len(scalars) + [spec for _, spec in pairs],
        out_specs=out_specs,
        scratch_shapes=list(scratch),
        input_output_aliases=alias or {},
        compiler_params=pltpu.CompilerParams(vmem_limit_bytes=limit),
        cost_estimate=pl.CostEstimate(flops=flops, bytes_accessed=2 * outs, transcendentals=0),
    )(*scalars, *(array for array, _ in pairs))


def swap(value, axis):
    return lax.ppermute(value, axis, [(0, 1), (1, 0)])


def hold(first, *others):
    return lax.optimization_barrier((first, *others))


def take_blocks(lower, groups):
    rows, columns = lower.shape[1], lower.shape[3]

    def kernel(lower_ref, *outs):
        for out, group in zip(outs, groups):
            for at, (i, j) in enumerate(group):
                out[at * rows : (at + 1) * rows, :] = lower_ref[i, :, j, :]

    shapes = [jax.ShapeDtypeStruct((len(g) * rows, columns), F32) for g in groups]
    return call(kernel, shapes, [], [lower])


def solve_part(half, inverse, k, right, at, partials):
    m, n = right[0].shape[0] // right[2], inverse[0].shape[1]
    width = right[0].shape[1]

    def kernel(half_ref, *refs):
        pieces, (b0, b1), parts = refs[:8], refs[8:10], refs[10 : 10 + len(partials)]
        out, inv, res = refs[10 + len(partials) :]
        for c in range(2):
            for y in range(2):
                off = half_ref[0] if y == 0 else 1 - half_ref[0]
                off = pl.multiple_of(off * n + c * 2 * n, n)
                for h in range(2):
                    inv[pl.ds(off, n), h * n : (h + 1) * n] = pieces[c * 4 + y * 2 + h][...]
        for h, b in enumerate((b0, b1)):
            value = b[...]
            for p in parts:
                total = p[0, h * m : (h + 1) * m, :]
                for i in range(1, p.shape[0]):
                    total = total + p[i, h * m : (h + 1) * m, :]
                value = value - total
            res[h * m : (h + 1) * m, :] = value

        @pl.loop(0, 4)
        def _(t):
            here = pl.ds(pl.multiple_of(t * n, n), n)
            out[here, :] = dot(inv[here, :], res[...])

    return call(
        kernel,
        jax.ShapeDtypeStruct((4 * n, width), F32),
        [half],
        [(p, (n, n), (k, 0)) for p in inverse]
        + [(b, (m, width), (at, 0)) for b in right[:2]]
        + list(partials),
        [pltpu.VMEM((4 * n, 2 * n), F32), pltpu.VMEM((2 * m, width), F32)],
        flops=2 * 4 * n * 2 * n * width,
    )


def lower_blocks(group, picks, rows):
    return [(g, (rows, g.shape[1]), (at, 0)) for pick in picks for at in pick for g in group]


def stack_products(refs, outer, rows, solved, left, right):
    columns = refs[0].shape[1]
    many = len(solved)
    for o in range(outer):
        for j in range(many):
            for h in range(2):
                for c in range(2):
                    at = (o * many + j) * 4 + h + 2 * c
                    left[o * 2 + h, j * 2 + c] = refs[at][...]
    for j, s in enumerate(solved):
        for c in range(2):
            right[j * 2 + c] = s[c * columns : (c + 1) * columns, :]

    def product(t):
        total = dot(left[t, 0], right[0])
        for i in range(1, 2 * many):
            total = total + dot(left[t, i], right[i])
        return total

    return product


def product_scratch(outer, rows, columns, many, width):
    return [
        pltpu.VMEM((outer * 2, many * 2, rows, columns), F32),
        pltpu.VMEM((many * 2, columns, width), F32),
    ]


def update_part(group, picks, solved, rows, copies=0):
    width, columns, outer = solved[0].shape[1], group[0].shape[1], len(picks)
    blocks = lower_blocks(group, picks, rows)

    def kernel(*refs):
        out, left, right = refs[-3:]
        product = stack_products(refs, outer, rows, refs[len(blocks) : -3], left, right)

        @pl.loop(0, outer * 2)
        def _(t):
            here = pl.ds(pl.multiple_of(t * rows, rows), rows)
            value = product(t)
            if copies:
                for i in range(copies):
                    out[i, here, :] = value
            else:
                out[here, :] = value

    size = (outer * 2 * rows, width)
    return call(
        kernel,
        jax.ShapeDtypeStruct((copies, *size) if copies else size, F32),
        [],
        blocks + list(solved),
        product_scratch(outer, rows, columns, len(solved), width),
        flops=2 * len(blocks) * rows * columns * width,
    )


def tail_part(yh, group, picks, solved, before, rows, n):
    width, columns = solved.shape[1], group[0].shape[1]
    blocks = lower_blocks(group, picks, rows)
    count, share = len(picks), rows // n

    def kernel(yh_ref, *refs):
        s, b = refs[len(blocks)], refs[len(blocks) + 1]
        out, left, right = refs[-3:]
        product = stack_products(refs, count, rows, [s], left, right)
        for h in range(2):
            at = yh_ref[0] if h == 0 else 1 - yh_ref[0]

            @pl.loop(0, count)
            def _(o, h=h, at=at):
                here = pl.ds(pl.multiple_of((o * 2 + h) * rows, rows), rows)
                value = b[here, :] + product(o * 2 + h)
                for d in range(n):
                    out[at * n + d, o] = value[d * share : (d + 1) * share]

    return call(
        kernel,
        jax.ShapeDtypeStruct((2 * n, count, share, width), F32),
        [yh],
        [*blocks, solved, before],
        product_scratch(count, rows, columns, 1, width),
        flops=2 * len(blocks) * rows * columns * width,
    )


def join_halves(first, second):
    size, width = first.shape[0] // 2, first.shape[1]

    def kernel(first_ref, second_ref, out_ref):
        out_ref[:size] = first_ref[...]
        out_ref[size:] = second_ref[...]

    arrays = [(first, (size, width), (0, 0)), (second, (size, width), (1, 0))]
    return call(kernel, jax.ShapeDtypeStruct(first.shape, F32), [], arrays)


def sum_groups(pieces, groups):
    def kernel(in_ref, out_ref):
        n = in_ref.shape[0] // groups
        for g in range(groups):
            total = in_ref[g * n]
            for i in range(1, n):
                total = total + in_ref[g * n + i]
            for i in range(n):
                out_ref[i, g] = total

    shape = (pieces.shape[0] // groups, groups, *pieces.shape[1:])
    return call(kernel, jax.ShapeDtypeStruct(shape, F32), [], [pieces], limit=8 << 20)


def sum_copies(pieces):
    def kernel(in_ref, out_ref):
        n = in_ref.shape[0]
        total = in_ref[0]
        for i in range(1, n):
            total = total + in_ref[i]
        for i in range(n):
            out_ref[i] = total

    return call(kernel, jax.ShapeDtypeStruct(pieces.shape, F32), [], [pieces], limit=8 << 20)


def place(yh, core, out, first, quarters, shape):
    rows, size = shape[1], quarters[0][0].shape[1]

    def kernel(yh_ref, core_ref, *refs):
        for k in range(len(quarters)):
            for h in range(2):
                for c in range(2):
                    p = yh_ref[0] if h == 0 else 1 - yh_ref[0]
                    q = core_ref[0] if c == 0 else 1 - core_ref[0]
                    lanes = pl.ds(pl.multiple_of((p * 2 + q) * size, size), size)
                    refs[-1][k, :, lanes] = refs[k * 2 + h][c * rows : (c + 1) * rows, :]

    arrays = [v for pair in quarters for v in pair]
    old = [] if out is None else [(out, pl.BlockSpec(memory_space=pl.ANY))]
    return call(
        kernel,
        jax.ShapeDtypeStruct(shape, F32),
        [yh, core],
        arrays + old,
        out_specs=block((len(quarters), *shape[1:]), first // len(quarters), 0, 0),
        alias=None if out is None else {2 + len(arrays): 0},
    )


def finish(core, pieces, right_side, first):
    _, rows, width = right_side.shape
    n, _, count, share, size = pieces[0].shape

    def kernel(core_ref, right_ref, *refs):
        for h in range(2):
            for c in range(2):
                q = core_ref[0] if c == 0 else 1 - core_ref[0]
                lanes = pl.ds(pl.multiple_of((h * 2 + q) * size, size), size)
                for d in range(n):
                    here = slice(d * share, (d + 1) * share)
                    refs[-1][:, here, lanes] = right_ref[:, here, lanes] - refs[c][d, h]

    return call(
        kernel,
        jax.ShapeDtypeStruct((count, rows, width), F32),
        [core],
        [(right_side, (count, rows, width), (first // count, 0, 0)), *pieces],
    )


def on_device(lower, inverse, right_side):
    chain, blocks = inverse.shape[0], right_side.shape[0]
    rows, width = right_side.shape[1:]
    part = width // 4
    yh, z, x, core, yl = (lax.axis_index(a).astype(jnp.int32) for a in AXES)
    nz, nx = lax.axis_size("z"), lax.axis_size("x")
    half, yh1, core1 = (v.reshape(1) for v in (yl, yh, core))

    def across(value):
        return [
            value,
            swap(value, "yh"),
            swap(value, "yl"),
            lax.ppermute(value, ("yh", "yl"), [(i, 3 - i) for i in range(4)]),
        ]

    def with_core(four):
        return four + [swap(v, "core") for v in four]

    def right_of(first, last):
        size = (last - first, rows, part)
        mine = lax.dynamic_slice(right_side, (first, 0, (yh * 2 + core) * part), size)
        send = lax.dynamic_slice(right_side, (first, 0, ((1 - yh) * 2 + core) * part), size)
        mine, send = (v.reshape(-1, part) for v in (mine, send))
        return mine, swap(send, "yh"), last - first

    def spread_lower(value):
        other = swap(value, "yh")
        return [value, other, swap(value, "core"), swap(other, "core")]

    flat = inverse.reshape(-1, inverse.shape[2])
    first_inverse = with_core(across(flat[:rows]))
    first_right = right_of(0, 1)
    rest_four = across(flat[rows:])
    rest_right = right_of(1, chain)

    group_of = [[(1, 0), (2, 0), (2, 1), (3, 0), (3, 1), (3, 2)]]
    group_of.append([(i, j) for i in range(chain, blocks) for j in range(chain)])
    near, far = (spread_lower(v) for v in take_blocks(lower, group_of))
    tails = [[i * chain + j for j in range(chain)] for i in range(blocks - chain)]

    def z_sum(value):
        return lax.all_to_all(value.reshape(nz, -1, part), "z", 0, 0)

    def z_all(value):
        return lax.all_to_all(sum_copies(value), "z", 0, 0).reshape(-1, part)

    def step(k, solved):
        picks = [[k * (k - 1) // 2 + j for j in range(k)]]
        return [lax.all_to_all(update_part(near, picks, solved, rows, nx), "x", 0, 0)]

    def quarters(unknowns):
        a = join_halves(unknowns, swap(unknowns, "core"))
        return a, swap(a, "yh")

    shape = (chain, lower.shape[3], width)

    summed = z_sum(solve_part(half, first_inverse, 0, first_right, 0, []))
    s0 = z_all(summed)
    s0, *held = hold(s0, *near, *rest_four)
    near, rest_four = held[:4], held[4:]
    rest_inverse = with_core(rest_four)

    parts = step(1, [s0])
    parts[0], *rest = hold(parts[0], *rest_inverse, rest_right[0], rest_right[1])
    rest_inverse, rest_right = rest[:-2], (*rest[-2:], rest_right[2])
    q0 = quarters(s0)
    s1 = z_all(z_sum(solve_part(half, rest_inverse, 0, rest_right, 0, parts)))
    s1, *q0 = hold(s1, *q0)

    parts = step(2, [s0, s1])
    q1 = quarters(s1)
    parts[0], *q1 = hold(parts[0], *q1)
    s2 = z_all(z_sum(solve_part(half, rest_inverse, 1, rest_right, 1, parts)))

    parts = step(3, [s0, s1, s2])
    parts[0], *far = hold(parts[0], *far)
    summed = z_sum(solve_part(half, rest_inverse, 2, rest_right, 2, parts))
    before = update_part(far, [t[:3] for t in tails], [s0, s1, s2], rows)
    q2 = quarters(s2)
    summed, before = hold(summed, before)
    s3 = z_all(summed)
    s3, *q2 = hold(s3, *q2)

    pieces = tail_part(yh1, far, [t[3:] for t in tails], s3, before, rows, nx)
    q3 = quarters(s3)
    own = lax.all_to_all(pieces, ("yh", "x"), 0, 0)
    out = place(yh1, core1, None, 0, [q0, q1, q2], shape)
    own, out = hold(own, out)
    final = lax.all_to_all(sum_groups(own, 2), "x", 0, 0)
    final, *q3 = hold(final, *q3)
    other = swap(final, "core")
    out = place(yh1, core1, out, 3, [q3], shape)
    return out, finish(core1, [final, other], right_side, chain)


def solution(mesh):
    fine = Mesh(mesh.devices.reshape(SIZES), AXES)
    return jax.shard_map(
        on_device,
        mesh=fine,
        in_specs=(
            P(None, ("yh", "z"), None, ("x", "core")),
            P(None, ("x", "core", "yl"), ("yh", "z")),
            P(None, ("yh", "z"), "yl"),
        ),
        out_specs=(P(None, ("x", "core"), "yl"), P(None, ("yh", "z"), "yl")),
        check_vma=False,
    )
```

```python
import jax
import jax.numpy as jnp
from jax import lax
from jax.experimental import pallas as pl
from jax.experimental.pallas import tpu as pltpu
from jax.sharding import Mesh
from jax.sharding import PartitionSpec as P

LIMIT = 60 << 20

AXES = ("yh", "z", "x", "core", "yl")
SIZES = (2, 8, 4, 2, 2)
F32 = jnp.float32
SMEM = pl.BlockSpec(memory_space=pltpu.SMEM)


def dot(a, b):
    return jnp.dot(a, b, precision=lax.Precision.HIGHEST, preferred_element_type=F32)


def block(shape, *at):
    return pl.BlockSpec(shape, lambda _: at, pipeline_mode=pl.Buffered(1))


def whole(array):
    return block(array.shape, *(0,) * len(array.shape))


def call(
    kernel, out_shape, scalars, arrays, scratch=(), flops=0, out_specs=None, alias=None, limit=LIMIT
):
    pairs = [a if isinstance(a, tuple) else (a, whole(a)) for a in arrays]
    pairs = [(p[0], block(p[1], *p[2])) if len(p) == 3 else p for p in pairs]
    many = isinstance(out_shape, list)
    if out_specs is None:
        out_specs = [whole(o) for o in out_shape] if many else whole(out_shape)
    outs = sum(4 * o.size for o in (out_shape if many else [out_shape]))
    return pl.pallas_call(
        kernel,
        grid=(1,),
        out_shape=out_shape,
        in_specs=[SMEM] * len(scalars) + [spec for _, spec in pairs],
        out_specs=out_specs,
        scratch_shapes=list(scratch),
        input_output_aliases=alias or {},
        compiler_params=pltpu.CompilerParams(vmem_limit_bytes=limit),
        cost_estimate=pl.CostEstimate(flops=flops, bytes_accessed=2 * outs, transcendentals=0),
    )(*scalars, *(array for array, _ in pairs))


def swap(value, axis):
    return lax.ppermute(value, axis, [(0, 1), (1, 0)])


def hold(first, *others):
    return lax.optimization_barrier((first, *others))


def take_blocks(lower, groups):
    rows, columns = lower.shape[1], lower.shape[3]

    def kernel(lower_ref, *outs):
        for out, group in zip(outs, groups):
            for at, (i, j) in enumerate(group):
                out[at * rows : (at + 1) * rows, :] = lower_ref[i, :, j, :]

    shapes = [jax.ShapeDtypeStruct((len(g) * rows, columns), F32) for g in groups]
    return call(kernel, shapes, [], [lower])


def solve_part(half, inverse, k, right, at, partials):
    m, n = right[0].shape[0] // right[2], inverse[0].shape[1]
    width = right[0].shape[1]

    def kernel(half_ref, *refs):
        pieces, (b0, b1), parts = refs[:8], refs[8:10], refs[10 : 10 + len(partials)]
        out, inv, res = refs[10 + len(partials) :]
        for c in range(2):
            for y in range(2):
                off = half_ref[0] if y == 0 else 1 - half_ref[0]
                off = pl.multiple_of(off * n + c * 2 * n, n)
                for h in range(2):
                    inv[pl.ds(off, n), h * n : (h + 1) * n] = pieces[c * 4 + y * 2 + h][...]
        for h, b in enumerate((b0, b1)):
            value = b[...]
            for p in parts:
                total = p[0, h * m : (h + 1) * m, :]
                for i in range(1, p.shape[0]):
                    total = total + p[i, h * m : (h + 1) * m, :]
                value = value - total
            res[h * m : (h + 1) * m, :] = value

        @pl.loop(0, 4)
        def _(t):
            here = pl.ds(pl.multiple_of(t * n, n), n)
            out[here, :] = dot(inv[here, :], res[...])

    return call(
        kernel,
        jax.ShapeDtypeStruct((4 * n, width), F32),
        [half],
        [(p, (n, n), (k, 0)) for p in inverse]
        + [(b, (m, width), (at, 0)) for b in right[:2]]
        + list(partials),
        [pltpu.VMEM((4 * n, 2 * n), F32), pltpu.VMEM((2 * m, width), F32)],
        flops=2 * 4 * n * 2 * n * width,
    )


def lower_blocks(group, picks, rows):
    return [(g, (rows, g.shape[1]), (at, 0)) for pick in picks for at in pick for g in group]


def stack_products(refs, outer, rows, solved, left, right):
    columns = refs[0].shape[1]
    many = len(solved)
    for o in range(outer):
        for j in range(many):
            for h in range(2):
                for c in range(2):
                    at = (o * many + j) * 4 + h + 2 * c
                    left[o * 2 + h, j * 2 + c] = refs[at][...]
    for j, s in enumerate(solved):
        for c in range(2):
            right[j * 2 + c] = s[c * columns : (c + 1) * columns, :]

    def product(t):
        total = dot(left[t, 0], right[0])
        for i in range(1, 2 * many):
            total = total + dot(left[t, i], right[i])
        return total

    return product


def product_scratch(outer, rows, columns, many, width):
    return [
        pltpu.VMEM((outer * 2, many * 2, rows, columns), F32),
        pltpu.VMEM((many * 2, columns, width), F32),
    ]


def update_part(group, picks, solved, rows, copies=0):
    width, columns, outer = solved[0].shape[1], group[0].shape[1], len(picks)
    blocks = lower_blocks(group, picks, rows)

    def kernel(*refs):
        out, left, right = refs[-3:]
        product = stack_products(refs, outer, rows, refs[len(blocks) : -3], left, right)

        @pl.loop(0, outer * 2)
        def _(t):
            here = pl.ds(pl.multiple_of(t * rows, rows), rows)
            value = product(t)
            if copies:
                for i in range(copies):
                    out[i, here, :] = value
            else:
                out[here, :] = value

    size = (outer * 2 * rows, width)
    return call(
        kernel,
        jax.ShapeDtypeStruct((copies, *size) if copies else size, F32),
        [],
        blocks + list(solved),
        product_scratch(outer, rows, columns, len(solved), width),
        flops=2 * len(blocks) * rows * columns * width,
    )


def tail_part(yh, group, picks, solved, before, rows, n):
    width, columns = solved.shape[1], group[0].shape[1]
    blocks = lower_blocks(group, picks, rows)
    count, share = len(picks), rows // n

    def kernel(yh_ref, *refs):
        s, b = refs[len(blocks)], refs[len(blocks) + 1]
        out, left, right = refs[-3:]
        product = stack_products(refs, count, rows, [s], left, right)
        for h in range(2):
            at = yh_ref[0] if h == 0 else 1 - yh_ref[0]

            @pl.loop(0, count)
            def _(o, h=h, at=at):
                here = pl.ds(pl.multiple_of((o * 2 + h) * rows, rows), rows)
                value = b[here, :] + product(o * 2 + h)
                for d in range(n):
                    out[at * n + d, o] = value[d * share : (d + 1) * share]

    return call(
        kernel,
        jax.ShapeDtypeStruct((2 * n, count, share, width), F32),
        [yh],
        [*blocks, solved, before],
        product_scratch(count, rows, columns, 1, width),
        flops=2 * len(blocks) * rows * columns * width,
    )


def join_halves(first, second):
    size, width = first.shape[0] // 2, first.shape[1]

    def kernel(first_ref, second_ref, out_ref):
        out_ref[:size] = first_ref[...]
        out_ref[size:] = second_ref[...]

    arrays = [(first, (size, width), (0, 0)), (second, (size, width), (1, 0))]
    return call(kernel, jax.ShapeDtypeStruct(first.shape, F32), [], arrays)


def sum_groups(pieces, groups):
    def kernel(in_ref, out_ref):
        n = in_ref.shape[0] // groups
        for g in range(groups):
            total = in_ref[g * n]
            for i in range(1, n):
                total = total + in_ref[g * n + i]
            for i in range(n):
                out_ref[i, g] = total

    shape = (pieces.shape[0] // groups, groups, *pieces.shape[1:])
    return call(kernel, jax.ShapeDtypeStruct(shape, F32), [], [pieces], limit=8 << 20)


def sum_copies(pieces):
    def kernel(in_ref, out_ref):
        n = in_ref.shape[0]
        total = in_ref[0]
        for i in range(1, n):
            total = total + in_ref[i]
        for i in range(n):
            out_ref[i] = total

    return call(kernel, jax.ShapeDtypeStruct(pieces.shape, F32), [], [pieces], limit=8 << 20)


def place(yh, core, out, first, quarters, shape):
    rows, size = shape[1], quarters[0][0].shape[1]

    def kernel(yh_ref, core_ref, *refs):
        for k in range(len(quarters)):
            for h in range(2):
                for c in range(2):
                    p = yh_ref[0] if h == 0 else 1 - yh_ref[0]
                    q = core_ref[0] if c == 0 else 1 - core_ref[0]
                    lanes = pl.ds(pl.multiple_of((p * 2 + q) * size, size), size)
                    refs[-1][k, :, lanes] = refs[k * 2 + h][c * rows : (c + 1) * rows, :]

    arrays = [v for pair in quarters for v in pair]
    old = [] if out is None else [(out, pl.BlockSpec(memory_space=pl.ANY))]
    return call(
        kernel,
        jax.ShapeDtypeStruct(shape, F32),
        [yh, core],
        arrays + old,
        out_specs=block((len(quarters), *shape[1:]), first // len(quarters), 0, 0),
        alias=None if out is None else {2 + len(arrays): 0},
    )


def finish(core, pieces, right_side, first):
    _, rows, width = right_side.shape
    n, _, count, share, size = pieces[0].shape

    def kernel(core_ref, right_ref, *refs):
        for h in range(2):
            for c in range(2):
                q = core_ref[0] if c == 0 else 1 - core_ref[0]
                lanes = pl.ds(pl.multiple_of((h * 2 + q) * size, size), size)
                for d in range(n):
                    here = slice(d * share, (d + 1) * share)
                    refs[-1][:, here, lanes] = right_ref[:, here, lanes] - refs[c][d, h]

    return call(
        kernel,
        jax.ShapeDtypeStruct((count, rows, width), F32),
        [core],
        [(right_side, (count, rows, width), (first // count, 0, 0)), *pieces],
        limit=16 << 20,
    )


def on_device(lower, inverse, right_side):
    chain, blocks = inverse.shape[0], right_side.shape[0]
    rows, width = right_side.shape[1:]
    part = width // 4
    yh, z, x, core, yl = (lax.axis_index(a).astype(jnp.int32) for a in AXES)
    nz, nx = lax.axis_size("z"), lax.axis_size("x")
    half, yh1, core1 = (v.reshape(1) for v in (yl, yh, core))

    def across(value):
        return [
            value,
            swap(value, "yh"),
            swap(value, "yl"),
            lax.ppermute(value, ("yh", "yl"), [(i, 3 - i) for i in range(4)]),
        ]

    def with_core(values):
        return [*values, *(swap(v, "core") for v in values)]

    def right_of(first, last):
        size = (last - first, rows, part)
        mine = lax.dynamic_slice(right_side, (first, 0, (yh * 2 + core) * part), size)
        send = lax.dynamic_slice(right_side, (first, 0, ((1 - yh) * 2 + core) * part), size)
        mine, send = (v.reshape(-1, part) for v in (mine, send))
        return mine, swap(send, "yh"), last - first

    def spread_yh(value):
        return [value, swap(value, "yh")]

    flat = inverse.reshape(-1, inverse.shape[2])
    first_inverse = with_core(across(flat[:rows]))
    first_right = right_of(0, 1)
    rest_four = across(flat[rows:])
    rest_right = right_of(1, chain)

    group_of = [[(1, 0)], [(2, 0), (2, 1), (3, 0), (3, 1), (3, 2)]]
    group_of.append([(i, j) for i in range(chain, blocks) for j in range(chain)])
    near, mid, far = (spread_yh(v) for v in take_blocks(lower, group_of))
    tails = [[i * chain + j for j in range(chain)] for i in range(blocks - chain)]

    def z_sum(value):
        return lax.all_to_all(value.reshape(nz, -1, part), "z", 0, 0)

    def z_all(value):
        return lax.all_to_all(sum_copies(value), "z", 0, 0).reshape(-1, part)

    def step(group, pick, solved):
        return lax.all_to_all(update_part(group, [pick], solved, rows, nx), "x", 0, 0)

    def joined(unknowns):
        return join_halves(unknowns, swap(unknowns, "core"))

    shape = (chain, lower.shape[3], width)

    summed = z_sum(solve_part(half, first_inverse, 0, first_right, 0, []))
    summed, near[1], *rest_four = hold(summed, near[1], *rest_four)
    near = with_core(near)
    rest_inverse = with_core(rest_four)
    s0 = z_all(summed)
    s0, *held = hold(s0, *near, *rest_inverse)
    near, rest_inverse = held[:4], held[4:]

    part_sums = step(near, [0], [s0])
    part_sums, right, mid[1] = hold(part_sums, rest_right[1], mid[1])
    rest_right = (rest_right[0], right, rest_right[2])
    summed = z_sum(solve_part(half, rest_inverse, 0, rest_right, 0, [part_sums]))
    mid = with_core(mid)
    j0 = joined(s0)
    summed, j0, *mid = hold(summed, j0, *mid)
    s1 = z_all(summed)
    q0 = (j0, swap(j0, "yh"))
    s1, *q0 = hold(s1, *q0)

    part_sums = step(mid, [0, 1], [s0, s1])
    j1 = joined(s1)
    part_sums, j1 = hold(part_sums, j1)
    q1 = (j1, swap(j1, "yh"))
    summed = z_sum(solve_part(half, rest_inverse, 1, rest_right, 1, [part_sums]))
    summed, *q1 = hold(summed, *q1)
    s2 = z_all(summed)

    part_sums = step(mid, [2, 3, 4], [s0, s1, s2])
    far = with_core(far)
    part_sums, *far = hold(part_sums, *far)
    summed = z_sum(solve_part(half, rest_inverse, 2, rest_right, 2, [part_sums]))
    before = update_part(far, [t[:3] for t in tails], [s0, s1, s2], rows)
    j2 = joined(s2)
    summed, before, j2 = hold(summed, before, j2)
    s3 = z_all(summed)
    q2 = (j2, swap(j2, "yh"))
    s3, *q2 = hold(s3, *q2)

    pieces = tail_part(yh1, far, [t[3:] for t in tails], s3, before, rows, nx)
    j3 = joined(s3)
    q3 = (j3, swap(j3, "yh"))
    own = lax.all_to_all(pieces, ("yh", "x"), 0, 0)
    out = place(yh1, core1, None, 0, [q0, q1, q2], shape)
    own, out = hold(own, out)
    final = lax.all_to_all(sum_groups(own, 2), "x", 0, 0)
    out = place(yh1, core1, out, 3, [q3], shape)
    return out, finish(core1, [final, swap(final, "core")], right_side, chain)


def solution(mesh):
    fine = Mesh(mesh.devices.reshape(SIZES), AXES)
    return jax.shard_map(
        on_device,
        mesh=fine,
        in_specs=(
            P(None, ("yh", "z"), None, ("x", "core")),
            P(None, ("x", "core", "yl"), ("yh", "z")),
            P(None, ("yh", "z"), "yl"),
        ),
        out_specs=(P(None, ("x", "core"), "yl"), P(None, ("yh", "z"), "yl")),
        check_vma=False,
    )
```

```python
import math

import jax
import jax.numpy as jnp
from jax import lax
from jax.experimental import pallas as pl
from jax.experimental.pallas import tpu as pltpu
from jax.sharding import Mesh
from jax.sharding import PartitionSpec as P

LIMIT = 60 << 20

AXES = ("yh", "z", "x", "core", "yl")
SIZES = (2, 8, 4, 2, 2)
F32 = jnp.float32
SMEM = pl.BlockSpec(memory_space=pltpu.SMEM)


def dot(a, b):
    return jnp.dot(a, b, precision=lax.Precision.HIGHEST, preferred_element_type=F32)


HERE = pl.BlockSpec(memory_space=pltpu.VMEM)


def block(shape, *at):
    return pl.BlockSpec(shape, lambda _: at, pipeline_mode=pl.Buffered(1))


def whole(array):
    return block(array.shape, *(0,) * len(array.shape))


def call(
    kernel, out_shape, scalars, arrays, scratch=(), flops=0, out_specs=None, alias=None, limit=LIMIT
):
    pairs = [a if isinstance(a, tuple) else (a, whole(a)) for a in arrays]
    pairs = [(p[0], block(p[1], *p[2])) if len(p) == 3 else p for p in pairs]
    pairs = [
        (pltpu.with_memory_space_constraint(array, pltpu.VMEM), spec) if spec is HERE else (array, spec)
        for array, spec in pairs
    ]
    many = isinstance(out_shape, list)
    if out_specs is None:
        out_specs = [whole(o) for o in out_shape] if many else whole(out_shape)
    outs = sum(4 * math.prod(o.shape) for o in (out_shape if many else [out_shape]))
    return pl.pallas_call(
        kernel,
        grid=(1,),
        out_shape=out_shape,
        in_specs=[SMEM] * len(scalars) + [spec for _, spec in pairs],
        out_specs=out_specs,
        scratch_shapes=list(scratch),
        input_output_aliases=alias or {},
        compiler_params=pltpu.CompilerParams(vmem_limit_bytes=limit),
        cost_estimate=pl.CostEstimate(flops=flops, bytes_accessed=2 * outs, transcendentals=0),
    )(*scalars, *(array for array, _ in pairs))


def swap(value, axis):
    return lax.ppermute(value, axis, [(0, 1), (1, 0)])


def hold(first, *others):
    return lax.optimization_barrier((first, *others))


def take_blocks(lower, groups):
    rows, columns = lower.shape[1], lower.shape[3]

    def kernel(lower_ref, *outs):
        for out, group in zip(outs, groups):
            for at, (i, j) in enumerate(group):
                out[at * rows : (at + 1) * rows, :] = lower_ref[i, :, j, :]

    shapes = [jax.ShapeDtypeStruct((len(g) * rows, columns), F32) for g in groups]
    return call(kernel, shapes, [], [lower])


def solve_part(half, inverse, k, right, at, partials):
    m, n = right[0].shape[0] // right[2], inverse[0].shape[1]
    width = right[0].shape[1]

    def kernel(half_ref, *refs):
        pieces, (b0, b1), parts = refs[:8], refs[8:10], refs[10 : 10 + len(partials)]
        out, inv, res = refs[10 + len(partials) :]
        for c in range(2):
            for y in range(2):
                off = half_ref[0] if y == 0 else 1 - half_ref[0]
                off = pl.multiple_of(off * n + c * 2 * n, n)
                for h in range(2):
                    inv[pl.ds(off, n), h * n : (h + 1) * n] = pieces[c * 4 + y * 2 + h][...]
        for h, b in enumerate((b0, b1)):
            value = b[...]
            for p in parts:
                total = p[0, h * m : (h + 1) * m, :]
                for i in range(1, p.shape[0]):
                    total = total + p[i, h * m : (h + 1) * m, :]
                value = value - total
            res[h * m : (h + 1) * m, :] = value

        @pl.loop(0, 4)
        def _(t):
            here = pl.ds(pl.multiple_of(t * n, n), n)
            out[here, :] = dot(inv[here, :], res[...])

    return call(
        kernel,
        jax.ShapeDtypeStruct((4 * n, width), F32),
        [half],
        [(p, (n, n), (k, 0)) for p in inverse]
        + [(b, (m, width), (at, 0)) for b in right[:2]]
        + [(p, HERE) for p in partials],
        [pltpu.VMEM((4 * n, 2 * n), F32), pltpu.VMEM((2 * m, width), F32)],
        flops=2 * 4 * n * 2 * n * width,
    )


def lower_blocks(group, picks, rows):
    return [(g, (rows, g.shape[1]), (at, 0)) for pick in picks for at in pick for g in group]


def stack_products(refs, outer, rows, solved, left, right):
    columns = refs[0].shape[1]
    many = len(solved)
    for o in range(outer):
        for j in range(many):
            for h in range(2):
                for c in range(2):
                    at = (o * many + j) * 4 + h + 2 * c
                    left[o * 2 + h, j * 2 + c] = refs[at][...]
    for j, s in enumerate(solved):
        for c in range(2):
            right[j * 2 + c] = s[c * columns : (c + 1) * columns, :]

    def product(t):
        total = dot(left[t, 0], right[0])
        for i in range(1, 2 * many):
            total = total + dot(left[t, i], right[i])
        return total

    return product


def product_scratch(outer, rows, columns, many, width):
    return [
        pltpu.VMEM((outer * 2, many * 2, rows, columns), F32),
        pltpu.VMEM((many * 2, columns, width), F32),
    ]


def update_part(group, picks, solved, rows, copies=0):
    width, columns, outer = solved[0].shape[1], group[0].shape[1], len(picks)
    blocks = lower_blocks(group, picks, rows)

    def kernel(*refs):
        out, left, right = refs[-3:]
        product = stack_products(refs, outer, rows, refs[len(blocks) : -3], left, right)

        @pl.loop(0, outer * 2)
        def _(t):
            here = pl.ds(pl.multiple_of(t * rows, rows), rows)
            value = product(t)
            if copies:
                for i in range(copies):
                    out[i, here, :] = value
            else:
                out[here, :] = value

    size = (outer * 2 * rows, width)
    return call(
        kernel,
        jax.ShapeDtypeStruct((copies, *size) if copies else size, F32),
        [],
        blocks + list(solved[:-1]) + [(solved[-1], HERE) if copies else solved[-1]],
        product_scratch(outer, rows, columns, len(solved), width),
        flops=2 * len(blocks) * rows * columns * width,
    )


def tail_part(yh, group, picks, solved, before, rows, n):
    width, columns = solved.shape[1], group[0].shape[1]
    blocks = lower_blocks(group, picks, rows)
    count, share = len(picks), rows // n

    def kernel(yh_ref, *refs):
        s, b = refs[len(blocks)], refs[len(blocks) + 1]
        out, left, right = refs[-3:]
        product = stack_products(refs, count, rows, [s], left, right)
        for h in range(2):
            at = yh_ref[0] if h == 0 else 1 - yh_ref[0]

            @pl.loop(0, count)
            def _(o, h=h, at=at):
                here = pl.ds(pl.multiple_of((o * 2 + h) * rows, rows), rows)
                value = b[here, :] + product(o * 2 + h)
                for d in range(n):
                    out[at * n + d, o] = value[d * share : (d + 1) * share]

    return call(
        kernel,
        jax.ShapeDtypeStruct((2 * n, count, share, width), F32),
        [yh],
        [*blocks, (solved, HERE), before],
        product_scratch(count, rows, columns, 1, width),
        flops=2 * len(blocks) * rows * columns * width,
    )


def join_halves(first, second):
    size, width = first.shape[0] // 2, first.shape[1]

    def kernel(first_ref, second_ref, out_ref):
        out_ref[:size] = first_ref[...]
        out_ref[size:] = second_ref[...]

    arrays = [(first, (size, width), (0, 0)), (second, (size, width), (1, 0))]
    return call(kernel, jax.ShapeDtypeStruct(first.shape, F32), [], arrays)


def sum_groups(pieces, groups):
    def kernel(in_ref, out_ref):
        n = in_ref.shape[0] // groups
        for g in range(groups):
            total = in_ref[g * n]
            for i in range(1, n):
                total = total + in_ref[g * n + i]
            for i in range(n):
                out_ref[i, g] = total

    shape = (pieces.shape[0] // groups, groups, *pieces.shape[1:])
    return call(kernel, pltpu.HBM(shape, F32), [], [(pieces, HERE)], limit=8 << 20)


def sum_copies(pieces):
    def kernel(in_ref, out_ref):
        n = in_ref.shape[0]
        total = in_ref[0]
        for i in range(1, n):
            total = total + in_ref[i]
        for i in range(n):
            out_ref[i] = total

    return call(kernel, pltpu.HBM(pieces.shape, F32), [], [(pieces, HERE)], limit=8 << 20)


def place(yh, core, out, first, quarters, shape):
    rows, size = shape[1], quarters[0][0].shape[1]

    def kernel(yh_ref, core_ref, *refs):
        for k in range(len(quarters)):
            for h in range(2):
                for c in range(2):
                    p = yh_ref[0] if h == 0 else 1 - yh_ref[0]
                    q = core_ref[0] if c == 0 else 1 - core_ref[0]
                    lanes = pl.ds(pl.multiple_of((p * 2 + q) * size, size), size)
                    refs[-1][k, :, lanes] = refs[k * 2 + h][c * rows : (c + 1) * rows, :]

    arrays = [v for pair in quarters for v in pair]
    old = [] if out is None else [(out, pl.BlockSpec(memory_space=pl.ANY))]
    return call(
        kernel,
        jax.ShapeDtypeStruct(shape, F32),
        [yh, core],
        arrays + old,
        out_specs=block((len(quarters), *shape[1:]), first // len(quarters), 0, 0),
        alias=None if out is None else {2 + len(arrays): 0},
    )


def finish(core, pieces, right_side, first):
    _, rows, width = right_side.shape
    n, _, count, share, size = pieces[0].shape

    def kernel(core_ref, right_ref, *refs):
        for h in range(2):
            for c in range(2):
                q = core_ref[0] if c == 0 else 1 - core_ref[0]
                lanes = pl.ds(pl.multiple_of((h * 2 + q) * size, size), size)
                for d in range(n):
                    here = slice(d * share, (d + 1) * share)
                    refs[-1][:, here, lanes] = right_ref[:, here, lanes] - refs[c][d, h]

    return call(
        kernel,
        jax.ShapeDtypeStruct((count, rows, width), F32),
        [core],
        [(right_side, (count, rows, width), (first // count, 0, 0)), *pieces],
        limit=16 << 20,
    )


def on_device(lower, inverse, right_side):
    chain, blocks = inverse.shape[0], right_side.shape[0]
    rows, width = right_side.shape[1:]
    part = width // 4
    yh, z, x, core, yl = (lax.axis_index(a).astype(jnp.int32) for a in AXES)
    nz, nx = lax.axis_size("z"), lax.axis_size("x")
    half, yh1, core1 = (v.reshape(1) for v in (yl, yh, core))

    def across(value):
        return [
            value,
            swap(value, "yh"),
            swap(value, "yl"),
            lax.ppermute(value, ("yh", "yl"), [(i, 3 - i) for i in range(4)]),
        ]

    def with_core(values):
        return [*values, *(swap(v, "core") for v in values)]

    def right_of(first, last):
        size = (last - first, rows, part)
        mine = lax.dynamic_slice(right_side, (first, 0, (yh * 2 + core) * part), size)
        send = lax.dynamic_slice(right_side, (first, 0, ((1 - yh) * 2 + core) * part), size)
        mine, send = (v.reshape(-1, part) for v in (mine, send))
        return mine, swap(send, "yh"), last - first

    def spread_yh(value):
        return [value, swap(value, "yh")]

    flat = inverse.reshape(-1, inverse.shape[2])
    first_inverse = with_core(across(flat[:rows]))
    first_right = right_of(0, 1)
    rest_four = across(flat[rows:])
    rest_right = right_of(1, chain)

    group_of = [[(1, 0)], [(2, 0), (2, 1), (3, 0), (3, 1), (3, 2)]]
    group_of.append([(i, j) for i in range(chain, blocks) for j in range(chain)])
    near, mid, far = (spread_yh(v) for v in take_blocks(lower, group_of))
    tails = [[i * chain + j for j in range(chain)] for i in range(blocks - chain)]

    def z_sum(value):
        return lax.all_to_all(value.reshape(nz, -1, part), "z", 0, 0)

    def z_all(value):
        return lax.all_to_all(sum_copies(value), "z", 0, 0).reshape(-1, part)

    def step(group, pick, solved):
        return lax.all_to_all(update_part(group, [pick], solved, rows, nx), "x", 0, 0)

    def joined(unknowns):
        return join_halves(unknowns, swap(unknowns, "core"))

    shape = (chain, lower.shape[3], width)

    summed = z_sum(solve_part(half, first_inverse, 0, first_right, 0, []))
    summed, near[1], *rest_four = hold(summed, near[1], *rest_four)
    near = with_core(near)
    rest_inverse = with_core(rest_four)
    s0 = z_all(summed)
    s0, *held = hold(s0, *near, *rest_inverse, rest_right[1])
    near, rest_inverse = held[:4], held[4:-1]
    rest_right = (rest_right[0], held[-1], rest_right[2])

    part_sums = step(near, [0], [s0])
    part_sums, mid[1] = hold(part_sums, mid[1])
    summed = z_sum(solve_part(half, rest_inverse, 0, rest_right, 0, [part_sums]))
    mid = with_core(mid)
    j0 = joined(s0)
    summed, j0, *mid = hold(summed, j0, *mid)
    s1 = z_all(summed)
    q0 = (j0, swap(j0, "yh"))
    s1, *q0 = hold(s1, *q0)

    part_sums = step(mid, [0, 1], [s0, s1])
    j1 = joined(s1)
    part_sums, j1 = hold(part_sums, j1)
    q1 = (j1, swap(j1, "yh"))
    summed = z_sum(solve_part(half, rest_inverse, 1, rest_right, 1, [part_sums]))
    summed, *q1 = hold(summed, *q1)
    s2 = z_all(summed)

    part_sums = step(mid, [2, 3, 4], [s0, s1, s2])
    far = with_core(far)
    part_sums, *far = hold(part_sums, *far)
    summed = z_sum(solve_part(half, rest_inverse, 2, rest_right, 2, [part_sums]))
    before = update_part(far, [t[:3] for t in tails], [s0, s1, s2], rows)
    j2 = joined(s2)
    summed, before, j2 = hold(summed, before, j2)
    s3 = z_all(summed)
    q2 = (j2, swap(j2, "yh"))
    s3, *q2 = hold(s3, *q2)

    pieces = tail_part(yh1, far, [t[3:] for t in tails], s3, before, rows, nx)
    j3 = joined(s3)
    own = lax.all_to_all(pieces, ("yh", "x"), 0, 0)
    out = place(yh1, core1, None, 0, [q0, q1, q2], shape)
    own, out, j3 = hold(own, out, j3)
    q3 = (j3, swap(j3, "yh"))
    final = lax.all_to_all(sum_groups(own, 2), "x", 0, 0)
    out = place(yh1, core1, out, 3, [q3], shape)
    return out, finish(core1, [final, swap(final, "core")], right_side, chain)


def solution(mesh):
    fine = Mesh(mesh.devices.reshape(SIZES), AXES)
    return jax.shard_map(
        on_device,
        mesh=fine,
        in_specs=(
            P(None, ("yh", "z"), None, ("x", "core")),
            P(None, ("x", "core", "yl"), ("yh", "z")),
            P(None, ("yh", "z"), "yl"),
        ),
        out_specs=(P(None, ("x", "core"), "yl"), P(None, ("yh", "z"), "yl")),
        check_vma=False,
    )
```

```python
import math

import jax
import jax.numpy as jnp
from jax import lax
from jax.experimental import pallas as pl
from jax.experimental.pallas import tpu as pltpu
from jax.sharding import Mesh
from jax.sharding import PartitionSpec as P

LIMIT = 60 << 20

AXES = ("yh", "z", "x", "core", "yl")
SIZES = (2, 8, 4, 2, 2)
F32 = jnp.float32
SMEM = pl.BlockSpec(memory_space=pltpu.SMEM)


def dot(a, b):
    return jnp.dot(a, b, precision=lax.Precision.HIGHEST, preferred_element_type=F32)


HERE = pl.BlockSpec(memory_space=pltpu.VMEM)


def block(shape, *at):
    return pl.BlockSpec(shape, lambda _: at, pipeline_mode=pl.Buffered(1))


def whole(array):
    return block(array.shape, *(0,) * len(array.shape))


def call(
    kernel, out_shape, scalars, arrays, scratch=(), flops=0, out_specs=None, alias=None, limit=LIMIT
):
    pairs = [a if isinstance(a, tuple) else (a, whole(a)) for a in arrays]
    pairs = [(p[0], block(p[1], *p[2])) if len(p) == 3 else p for p in pairs]
    pairs = [
        (pltpu.with_memory_space_constraint(array, pltpu.VMEM), spec) if spec is HERE else (array, spec)
        for array, spec in pairs
    ]
    many = isinstance(out_shape, list)
    if out_specs is None:
        out_specs = [whole(o) for o in out_shape] if many else whole(out_shape)
    outs = sum(4 * math.prod(o.shape) for o in (out_shape if many else [out_shape]))
    return pl.pallas_call(
        kernel,
        grid=(1,),
        out_shape=out_shape,
        in_specs=[SMEM] * len(scalars) + [spec for _, spec in pairs],
        out_specs=out_specs,
        scratch_shapes=list(scratch),
        input_output_aliases=alias or {},
        compiler_params=pltpu.CompilerParams(vmem_limit_bytes=limit),
        cost_estimate=pl.CostEstimate(flops=flops, bytes_accessed=2 * outs, transcendentals=0),
    )(*scalars, *(array for array, _ in pairs))


def swap(value, axis):
    return lax.ppermute(value, axis, [(0, 1), (1, 0)])


def hold(first, *others):
    return lax.optimization_barrier((first, *others))


def take_blocks(lower, groups):
    rows, columns = lower.shape[1], lower.shape[3]

    def kernel(lower_ref, *outs):
        for out, group in zip(outs, groups):
            for at, (i, j) in enumerate(group):
                out[at * rows : (at + 1) * rows, :] = lower_ref[i, :, j, :]

    shapes = [jax.ShapeDtypeStruct((len(g) * rows, columns), F32) for g in groups]
    return call(kernel, shapes, [], [lower])


def solve_part(half, inverse, k, right, at, partials):
    m, n = right[0].shape[0] // right[2], inverse[0].shape[1]
    width = right[0].shape[1]

    def kernel(half_ref, *refs):
        pieces, (b0, b1), parts = refs[:8], refs[8:10], refs[10 : 10 + len(partials)]
        out, inv, res = refs[10 + len(partials) :]
        for c in range(2):
            for y in range(2):
                off = half_ref[0] if y == 0 else 1 - half_ref[0]
                off = pl.multiple_of(off * n + c * 2 * n, n)
                for h in range(2):
                    inv[pl.ds(off, n), h * n : (h + 1) * n] = pieces[c * 4 + y * 2 + h][...]
        for h, b in enumerate((b0, b1)):
            value = b[...]
            for p in parts:
                total = p[0, h * m : (h + 1) * m, :]
                for i in range(1, p.shape[0]):
                    total = total + p[i, h * m : (h + 1) * m, :]
                value = value - total
            res[h * m : (h + 1) * m, :] = value

        @pl.loop(0, 4)
        def _(t):
            here = pl.ds(pl.multiple_of(t * n, n), n)
            out[here, :] = dot(inv[here, :], res[...])

    return call(
        kernel,
        jax.ShapeDtypeStruct((4 * n, width), F32),
        [half],
        [(p, (n, n), (k, 0)) for p in inverse]
        + [(b, (m, width), (at, 0)) for b in right[:2]]
        + [(p, HERE) for p in partials],
        [pltpu.VMEM((4 * n, 2 * n), F32), pltpu.VMEM((2 * m, width), F32)],
        flops=2 * 4 * n * 2 * n * width,
    )


def lower_blocks(group, picks, rows):
    return [(g, (rows, g.shape[1]), (at, 0)) for pick in picks for at in pick for g in group]


def stack_products(refs, outer, rows, solved, left, right):
    columns = refs[0].shape[1]
    many = len(solved)
    for o in range(outer):
        for j in range(many):
            for h in range(2):
                for c in range(2):
                    at = (o * many + j) * 4 + h + 2 * c
                    left[o * 2 + h, j * 2 + c] = refs[at][...]
    for j, s in enumerate(solved):
        for c in range(2):
            right[j * 2 + c] = s[c * columns : (c + 1) * columns, :]

    def product(t):
        total = dot(left[t, 0], right[0])
        for i in range(1, 2 * many):
            total = total + dot(left[t, i], right[i])
        return total

    return product


def product_scratch(outer, rows, columns, many, width):
    return [
        pltpu.VMEM((outer * 2, many * 2, rows, columns), F32),
        pltpu.VMEM((many * 2, columns, width), F32),
    ]


def update_part(group, picks, solved, rows, copies=0, before=None):
    width, columns, outer = solved[0].shape[1], group[0].shape[1], len(picks)
    blocks = lower_blocks(group, picks, rows)

    def kernel(*refs):
        out, left, right = refs[-3:]
        many = len(blocks) + len(solved)
        product = stack_products(refs, outer, rows, refs[len(blocks) : many], left, right)

        @pl.loop(0, outer * 2)
        def _(t):
            here = pl.ds(pl.multiple_of(t * rows, rows), rows)
            value = product(t)
            if before is not None:
                value = refs[many][here, :] + value
            if copies:
                for i in range(copies):
                    out[i, here, :] = value
            else:
                out[here, :] = value

    size = (outer * 2 * rows, width)
    return call(
        kernel,
        jax.ShapeDtypeStruct((copies, *size) if copies else size, F32),
        [],
        blocks
        + list(solved[:-1])
        + [(solved[-1], HERE) if copies else solved[-1]]
        + ([] if before is None else [before]),
        product_scratch(outer, rows, columns, len(solved), width),
        flops=2 * len(blocks) * rows * columns * width,
    )


def tail_part(yh, group, picks, solved, before, rows, n):
    width, columns = solved.shape[1], group[0].shape[1]
    blocks = lower_blocks(group, picks, rows)
    count, share = len(picks), rows // n

    def kernel(yh_ref, *refs):
        s, b = refs[len(blocks)], refs[len(blocks) + 1]
        out, left, right = refs[-3:]
        product = stack_products(refs, count, rows, [s], left, right)
        for h in range(2):
            at = yh_ref[0] if h == 0 else 1 - yh_ref[0]

            @pl.loop(0, count)
            def _(o, h=h, at=at):
                here = pl.ds(pl.multiple_of((o * 2 + h) * rows, rows), rows)
                value = b[here, :] + product(o * 2 + h)
                for d in range(n):
                    out[at * n + d, o] = value[d * share : (d + 1) * share]

    return call(
        kernel,
        jax.ShapeDtypeStruct((2 * n, count, share, width), F32),
        [yh],
        [*blocks, (solved, HERE), before],
        product_scratch(count, rows, columns, 1, width),
        flops=2 * len(blocks) * rows * columns * width,
    )


def join_halves(first, second):
    size, width = first.shape[0] // 2, first.shape[1]

    def kernel(first_ref, second_ref, out_ref):
        out_ref[:size] = first_ref[...]
        out_ref[size:] = second_ref[...]

    arrays = [(first, (size, width), (0, 0)), (second, (size, width), (1, 0))]
    return call(kernel, jax.ShapeDtypeStruct(first.shape, F32), [], arrays)


def sum_groups(pieces, groups):
    def kernel(in_ref, out_ref):
        n = in_ref.shape[0] // groups
        for g in range(groups):
            total = in_ref[g * n]
            for i in range(1, n):
                total = total + in_ref[g * n + i]
            for i in range(n):
                out_ref[i, g] = total

    shape = (pieces.shape[0] // groups, groups, *pieces.shape[1:])
    return call(kernel, pltpu.HBM(shape, F32), [], [(pieces, HERE)], limit=8 << 20)


def sum_copies(pieces):
    def kernel(in_ref, out_ref):
        n = in_ref.shape[0]
        total = in_ref[0]
        for i in range(1, n):
            total = total + in_ref[i]
        for i in range(n):
            out_ref[i] = total

    return call(kernel, pltpu.HBM(pieces.shape, F32), [], [(pieces, HERE)], limit=8 << 20)


def place(yh, core, out, first, quarters, shape):
    rows, size = shape[1], quarters[0][0].shape[1]

    def kernel(yh_ref, core_ref, *refs):
        for k in range(len(quarters)):
            for h in range(2):
                for c in range(2):
                    p = yh_ref[0] if h == 0 else 1 - yh_ref[0]
                    q = core_ref[0] if c == 0 else 1 - core_ref[0]
                    lanes = pl.ds(pl.multiple_of((p * 2 + q) * size, size), size)
                    refs[-1][k, :, lanes] = refs[k * 2 + h][c * rows : (c + 1) * rows, :]

    arrays = [v for pair in quarters for v in pair]
    old = [] if out is None else [(out, pl.BlockSpec(memory_space=pl.ANY))]
    return call(
        kernel,
        jax.ShapeDtypeStruct(shape, F32),
        [yh, core],
        arrays + old,
        out_specs=block((len(quarters), *shape[1:]), first // len(quarters), 0, 0),
        alias=None if out is None else {2 + len(arrays): 0},
    )


def finish(core, pieces, right_side, first):
    _, rows, width = right_side.shape
    n, _, count, share, size = pieces[0].shape

    def kernel(core_ref, right_ref, *refs):
        for h in range(2):
            for c in range(2):
                q = core_ref[0] if c == 0 else 1 - core_ref[0]
                lanes = pl.ds(pl.multiple_of((h * 2 + q) * size, size), size)
                for d in range(n):
                    here = slice(d * share, (d + 1) * share)
                    refs[-1][:, here, lanes] = right_ref[:, here, lanes] - refs[c][d, h]

    return call(
        kernel,
        jax.ShapeDtypeStruct((count, rows, width), F32),
        [core],
        [(right_side, (count, rows, width), (first // count, 0, 0)), *pieces],
        limit=16 << 20,
    )


def on_device(lower, inverse, right_side):
    chain, blocks = inverse.shape[0], right_side.shape[0]
    rows, width = right_side.shape[1:]
    part = width // 4
    yh, z, x, core, yl = (lax.axis_index(a).astype(jnp.int32) for a in AXES)
    nz, nx = lax.axis_size("z"), lax.axis_size("x")
    half, yh1, core1 = (v.reshape(1) for v in (yl, yh, core))

    def across(value):
        return [
            value,
            swap(value, "yh"),
            swap(value, "yl"),
            lax.ppermute(value, ("yh", "yl"), [(i, 3 - i) for i in range(4)]),
        ]

    def with_core(values):
        return [*values, *(swap(v, "core") for v in values)]

    def right_of(first, last):
        size = (last - first, rows, part)
        mine = lax.dynamic_slice(right_side, (first, 0, (yh * 2 + core) * part), size)
        send = lax.dynamic_slice(right_side, (first, 0, ((1 - yh) * 2 + core) * part), size)
        mine, send = (v.reshape(-1, part) for v in (mine, send))
        return mine, swap(send, "yh"), last - first

    def spread_yh(value):
        return [value, swap(value, "yh")]

    flat = inverse.reshape(-1, inverse.shape[2])
    first_inverse = with_core(across(flat[:rows]))
    first_right = right_of(0, 1)
    rest_four = across(flat[rows:])
    rest_right = right_of(1, chain)

    group_of = [[(1, 0)], [(2, 0), (2, 1), (3, 0), (3, 1), (3, 2)]]
    group_of.append([(i, j) for i in range(chain, blocks) for j in range(chain)])
    near, mid, far = (spread_yh(v) for v in take_blocks(lower, group_of))
    tails = [[i * chain + j for j in range(chain)] for i in range(blocks - chain)]

    def z_sum(value):
        return lax.all_to_all(value.reshape(nz, -1, part), "z", 0, 0)

    def z_all(value):
        return lax.all_to_all(sum_copies(value), "z", 0, 0).reshape(-1, part)

    def step(group, pick, solved, before=None):
        return lax.all_to_all(update_part(group, [pick], solved, rows, nx, before), "x", 0, 0)

    def joined(unknowns):
        return join_halves(unknowns, swap(unknowns, "core"))

    shape = (chain, lower.shape[3], width)

    summed = z_sum(solve_part(half, first_inverse, 0, first_right, 0, []))
    summed, near[1], *rest_four = hold(summed, near[1], *rest_four)
    near = with_core(near)
    rest_inverse = with_core(rest_four)
    s0 = z_all(summed)
    s0, *held = hold(s0, *near, *rest_inverse, rest_right[1])
    near, rest_inverse = held[:4], held[4:-1]
    rest_right = (rest_right[0], held[-1], rest_right[2])

    part_sums = step(near, [0], [s0])
    part_sums, mid[1] = hold(part_sums, mid[1])
    summed = z_sum(solve_part(half, rest_inverse, 0, rest_right, 0, [part_sums]))
    mid = with_core(mid)
    j0 = joined(s0)
    summed, j0, *mid = hold(summed, j0, *mid)
    s1 = z_all(summed)
    q0 = (j0, swap(j0, "yh"))
    ahead = update_part(mid, [[0]], [s0], rows)
    s1, ahead, *q0 = hold(s1, ahead, *q0)

    part_sums = step(mid, [1], [s1], ahead)
    j1 = joined(s1)
    part_sums, j1 = hold(part_sums, j1)
    q1 = (j1, swap(j1, "yh"))
    summed = z_sum(solve_part(half, rest_inverse, 1, rest_right, 1, [part_sums]))
    summed, *q1 = hold(summed, *q1)
    s2 = z_all(summed)
    ahead = update_part(mid, [[2, 3]], [s0, s1], rows)
    s2, ahead = hold(s2, ahead)

    part_sums = step(mid, [4], [s2], ahead)
    far = with_core(far)
    j2 = joined(s2)
    part_sums, j2, *far = hold(part_sums, j2, *far)
    summed = z_sum(solve_part(half, rest_inverse, 2, rest_right, 2, [part_sums]))
    before = update_part(far, [t[:3] for t in tails], [s0, s1, s2], rows)
    q2 = (j2, swap(j2, "yh"))
    summed, before, *q2 = hold(summed, before, *q2)
    s3 = z_all(summed)

    pieces = tail_part(yh1, far, [t[3:] for t in tails], s3, before, rows, nx)
    j3 = joined(s3)
    q3 = (j3, swap(j3, "yh"))
    own = lax.all_to_all(pieces, ("yh", "x"), 0, 0)
    out = place(yh1, core1, None, 0, [q0, q1, q2], shape)
    own, out = hold(own, out)
    final = lax.all_to_all(sum_groups(own, 2), "x", 0, 0)
    final, *q3 = hold(final, *q3)
    out = place(yh1, core1, out, 3, [q3], shape)
    return out, finish(core1, [final, swap(final, "core")], right_side, chain)


def solution(mesh):
    fine = Mesh(mesh.devices.reshape(SIZES), AXES)
    return jax.shard_map(
        on_device,
        mesh=fine,
        in_specs=(
            P(None, ("yh", "z"), None, ("x", "core")),
            P(None, ("x", "core", "yl"), ("yh", "z")),
            P(None, ("yh", "z"), "yl"),
        ),
        out_specs=(P(None, ("x", "core"), "yl"), P(None, ("yh", "z"), "yl")),
        check_vma=False,
    )
```

```python
import math

import jax
import jax.numpy as jnp
from jax import lax
from jax.experimental import pallas as pl
from jax.experimental.pallas import tpu as pltpu
from jax.sharding import Mesh
from jax.sharding import PartitionSpec as P

LIMIT = 60 << 20

AXES = ("yh", "z", "x", "core", "yl")
SIZES = (2, 8, 4, 2, 2)
F32 = jnp.float32
SMEM = pl.BlockSpec(memory_space=pltpu.SMEM)


def dot(a, b):
    return jnp.dot(a, b, precision=lax.Precision.HIGHEST, preferred_element_type=F32)


HERE = pl.BlockSpec(memory_space=pltpu.VMEM)


def block(shape, *at):
    return pl.BlockSpec(shape, lambda _: at, pipeline_mode=pl.Buffered(1))


def whole(array):
    return block(array.shape, *(0,) * len(array.shape))


def call(
    kernel, out_shape, scalars, arrays, scratch=(), flops=0, out_specs=None, alias=None, limit=LIMIT
):
    pairs = [a if isinstance(a, tuple) else (a, whole(a)) for a in arrays]
    pairs = [(p[0], block(p[1], *p[2])) if len(p) == 3 else p for p in pairs]
    pairs = [
        (pltpu.with_memory_space_constraint(array, pltpu.VMEM), spec) if spec is HERE else (array, spec)
        for array, spec in pairs
    ]
    many = isinstance(out_shape, list)
    if out_specs is None:
        out_specs = [whole(o) for o in out_shape] if many else whole(out_shape)
    outs = sum(4 * math.prod(o.shape) for o in (out_shape if many else [out_shape]))
    return pl.pallas_call(
        kernel,
        grid=(1,),
        out_shape=out_shape,
        in_specs=[SMEM] * len(scalars) + [spec for _, spec in pairs],
        out_specs=out_specs,
        scratch_shapes=list(scratch),
        input_output_aliases=alias or {},
        compiler_params=pltpu.CompilerParams(vmem_limit_bytes=limit),
        cost_estimate=pl.CostEstimate(flops=flops, bytes_accessed=2 * outs, transcendentals=0),
    )(*scalars, *(array for array, _ in pairs))


def swap(value, axis):
    return lax.ppermute(value, axis, [(0, 1), (1, 0)])


def hold(first, *others):
    return lax.optimization_barrier((first, *others))


def take_blocks(lower, groups):
    rows, columns = lower.shape[1], lower.shape[3]

    def kernel(lower_ref, *outs):
        for out, group in zip(outs, groups):
            for at, (i, j) in enumerate(group):
                out[at * rows : (at + 1) * rows, :] = lower_ref[i, :, j, :]

    shapes = [jax.ShapeDtypeStruct((len(g) * rows, columns), F32) for g in groups]
    return call(kernel, shapes, [], [lower])


def solve_part(half, inverse, k, right, at, partials):
    m, n = right[0].shape[0] // right[2], inverse[0].shape[1]
    width = right[0].shape[1]

    def kernel(half_ref, *refs):
        pieces, (b0, b1), parts = refs[:8], refs[8:10], refs[10 : 10 + len(partials)]
        out, inv, res = refs[10 + len(partials) :]
        for c in range(2):
            for y in range(2):
                off = half_ref[0] if y == 0 else 1 - half_ref[0]
                off = pl.multiple_of(off * n + c * 2 * n, n)
                for h in range(2):
                    inv[pl.ds(off, n), h * n : (h + 1) * n] = pieces[c * 4 + y * 2 + h][...]
        for h, b in enumerate((b0, b1)):
            value = b[...]
            for p in parts:
                total = p[0, h * m : (h + 1) * m, :]
                for i in range(1, p.shape[0]):
                    total = total + p[i, h * m : (h + 1) * m, :]
                value = value - total
            res[h * m : (h + 1) * m, :] = value

        @pl.loop(0, 4)
        def _(t):
            here = pl.ds(pl.multiple_of(t * n, n), n)
            out[here, :] = dot(inv[here, :], res[...])

    return call(
        kernel,
        jax.ShapeDtypeStruct((4 * n, width), F32),
        [half],
        [(p, (n, n), (k, 0)) for p in inverse]
        + [(b, (m, width), (at, 0)) for b in right[:2]]
        + [(p, HERE) for p in partials],
        [pltpu.VMEM((4 * n, 2 * n), F32), pltpu.VMEM((2 * m, width), F32)],
        flops=2 * 4 * n * 2 * n * width,
    )


def lower_blocks(group, picks, rows):
    return [(g, (rows, g.shape[1]), (at, 0)) for pick in picks for at in pick for g in group]


def stack_products(refs, outer, rows, solved, left, right):
    columns = refs[0].shape[1]
    many = len(solved)
    for o in range(outer):
        for j in range(many):
            for h in range(2):
                for c in range(2):
                    at = (o * many + j) * 4 + h + 2 * c
                    left[o * 2 + h, j * 2 + c] = refs[at][...]
    for j, s in enumerate(solved):
        for c in range(2):
            right[j * 2 + c] = s[c * columns : (c + 1) * columns, :]

    def product(t):
        total = dot(left[t, 0], right[0])
        for i in range(1, 2 * many):
            total = total + dot(left[t, i], right[i])
        return total

    return product


def product_scratch(outer, rows, columns, many, width):
    return [
        pltpu.VMEM((outer * 2, many * 2, rows, columns), F32),
        pltpu.VMEM((many * 2, columns, width), F32),
    ]


def update_part(group, picks, solved, rows, copies=0, before=None):
    width, columns, outer = solved[0].shape[1], group[0].shape[1], len(picks)
    blocks = lower_blocks(group, picks, rows)

    def kernel(*refs):
        out, left, right = refs[-3:]
        many = len(blocks) + len(solved)
        product = stack_products(refs, outer, rows, refs[len(blocks) : many], left, right)

        @pl.loop(0, outer * 2)
        def _(t):
            here = pl.ds(pl.multiple_of(t * rows, rows), rows)
            value = product(t)
            if before is not None:
                value = refs[many][here, :] + value
            if copies:
                for i in range(copies):
                    out[i, here, :] = value
            else:
                out[here, :] = value

    size = (outer * 2 * rows, width)
    return call(
        kernel,
        jax.ShapeDtypeStruct((copies, *size) if copies else size, F32),
        [],
        blocks
        + list(solved[:-1])
        + [(solved[-1], HERE) if copies else solved[-1]]
        + ([] if before is None else [before]),
        product_scratch(outer, rows, columns, len(solved), width),
        flops=2 * len(blocks) * rows * columns * width,
    )


def tail_part(yh, group, picks, solved, before, rows, n):
    width, columns = solved.shape[1], group[0].shape[1]
    blocks = lower_blocks(group, picks, rows)
    count, share = len(picks), rows // n

    def kernel(yh_ref, *refs):
        s, b = refs[len(blocks)], refs[len(blocks) + 1]
        out, left, right = refs[-3:]
        product = stack_products(refs, count, rows, [s], left, right)
        for h in range(2):
            at = yh_ref[0] if h == 0 else 1 - yh_ref[0]

            @pl.loop(0, count)
            def _(o, h=h, at=at):
                here = pl.ds(pl.multiple_of((o * 2 + h) * rows, rows), rows)
                value = b[here, :] + product(o * 2 + h)
                for d in range(n):
                    out[at * n + d, o] = value[d * share : (d + 1) * share]

    return call(
        kernel,
        jax.ShapeDtypeStruct((2 * n, count, share, width), F32),
        [yh],
        [*blocks, (solved, HERE), before],
        product_scratch(count, rows, columns, 1, width),
        flops=2 * len(blocks) * rows * columns * width,
    )


def join_halves(first, second):
    size, width = first.shape[0] // 2, first.shape[1]

    def kernel(first_ref, second_ref, out_ref):
        out_ref[:size] = first_ref[...]
        out_ref[size:] = second_ref[...]

    arrays = [(first, (size, width), (0, 0)), (second, (size, width), (1, 0))]
    return call(kernel, jax.ShapeDtypeStruct(first.shape, F32), [], arrays)


def sum_groups(pieces, groups):
    def kernel(in_ref, out_ref):
        n = in_ref.shape[0] // groups
        for g in range(groups):
            total = in_ref[g * n]
            for i in range(1, n):
                total = total + in_ref[g * n + i]
            for i in range(n):
                out_ref[i, g] = total

    shape = (pieces.shape[0] // groups, groups, *pieces.shape[1:])
    return call(kernel, pltpu.HBM(shape, F32), [], [(pieces, HERE)], limit=8 << 20)


def sum_copies(pieces):
    def kernel(in_ref, out_ref):
        n = in_ref.shape[0]
        total = in_ref[0]
        for i in range(1, n):
            total = total + in_ref[i]
        for i in range(n):
            out_ref[i] = total

    return call(kernel, pltpu.HBM(pieces.shape, F32), [], [(pieces, HERE)], limit=8 << 20)


def place(yh, core, out, first, quarters, shape):
    rows, size = shape[1], quarters[0][0].shape[1]

    def kernel(yh_ref, core_ref, *refs):
        for k in range(len(quarters)):
            for h in range(2):
                for c in range(2):
                    p = yh_ref[0] if h == 0 else 1 - yh_ref[0]
                    q = core_ref[0] if c == 0 else 1 - core_ref[0]
                    lanes = pl.ds(pl.multiple_of((p * 2 + q) * size, size), size)
                    refs[-1][k, :, lanes] = refs[k * 2 + h][c * rows : (c + 1) * rows, :]

    arrays = [v for pair in quarters for v in pair]
    old = [] if out is None else [(out, pl.BlockSpec(memory_space=pl.ANY))]
    return call(
        kernel,
        jax.ShapeDtypeStruct(shape, F32),
        [yh, core],
        arrays + old,
        out_specs=block((len(quarters), *shape[1:]), first // len(quarters), 0, 0),
        alias=None if out is None else {2 + len(arrays): 0},
    )


def finish(core, pieces, right_side, first):
    _, rows, width = right_side.shape
    n, _, count, share, size = pieces[0].shape

    def kernel(core_ref, right_ref, *refs):
        for h in range(2):
            for c in range(2):
                q = core_ref[0] if c == 0 else 1 - core_ref[0]
                lanes = pl.ds(pl.multiple_of((h * 2 + q) * size, size), size)
                for d in range(n):
                    here = slice(d * share, (d + 1) * share)
                    refs[-1][:, here, lanes] = right_ref[:, here, lanes] - refs[c][d, h]

    return call(
        kernel,
        jax.ShapeDtypeStruct((count, rows, width), F32),
        [core],
        [(right_side, (count, rows, width), (first // count, 0, 0)), *pieces],
        limit=16 << 20,
    )


def on_device(lower, inverse, right_side):
    chain, blocks = inverse.shape[0], right_side.shape[0]
    rows, width = right_side.shape[1:]
    part = width // 4
    yh, z, x, core, yl = (lax.axis_index(a).astype(jnp.int32) for a in AXES)
    nz, nx = lax.axis_size("z"), lax.axis_size("x")
    half, yh1, core1 = (v.reshape(1) for v in (yl, yh, core))

    def across(value):
        return [
            value,
            swap(value, "yh"),
            swap(value, "yl"),
            lax.ppermute(value, ("yh", "yl"), [(i, 3 - i) for i in range(4)]),
        ]

    def with_core(values):
        return [*values, *(swap(v, "core") for v in values)]

    def right_of(first, last):
        size = (last - first, rows, part)
        mine = lax.dynamic_slice(right_side, (first, 0, (yh * 2 + core) * part), size)
        send = lax.dynamic_slice(right_side, (first, 0, ((1 - yh) * 2 + core) * part), size)
        mine, send = (v.reshape(-1, part) for v in (mine, send))
        return mine, swap(send, "yh"), last - first

    def spread_yh(value):
        return [value, swap(value, "yh")]

    flat = inverse.reshape(-1, inverse.shape[2])
    first_inverse = with_core(across(flat[:rows]))
    first_right = right_of(0, 1)
    rest_four = across(flat[rows:])
    rest_right = right_of(1, chain)

    group_of = [[(1, 0)], [(2, 0), (2, 1), (3, 0), (3, 1), (3, 2)]]
    group_of.append([(i, j) for i in range(chain, blocks) for j in range(chain)])
    near, mid, far = (spread_yh(v) for v in take_blocks(lower, group_of))
    tails = [[i * chain + j for j in range(chain)] for i in range(blocks - chain)]

    def z_sum(value):
        return lax.all_to_all(value.reshape(nz, -1, part), "z", 0, 0)

    def z_all(value):
        return lax.all_to_all(sum_copies(value), "z", 0, 0).reshape(-1, part)

    def step(group, pick, solved, before=None):
        return lax.all_to_all(update_part(group, [pick], solved, rows, nx, before), "x", 0, 0)

    def joined(unknowns):
        return join_halves(unknowns, swap(unknowns, "core"))

    shape = (chain, lower.shape[3], width)

    summed = z_sum(solve_part(half, first_inverse, 0, first_right, 0, []))
    summed, near[1], *rest_four = hold(summed, near[1], *rest_four)
    near = with_core(near)
    rest_inverse = with_core(rest_four)
    s0 = z_all(summed)
    s0, *held = hold(s0, *near, *rest_inverse, rest_right[1])
    near, rest_inverse = held[:4], held[4:-1]
    rest_right = (rest_right[0], held[-1], rest_right[2])

    part_sums = step(near, [0], [s0])
    summed = z_sum(solve_part(half, rest_inverse, 0, rest_right, 0, [part_sums]))
    j0 = joined(s0)
    summed, j0, mid[1] = hold(summed, j0, mid[1])
    mid = with_core(mid)
    s1 = z_all(summed)
    q0 = (j0, swap(j0, "yh"))
    ahead = update_part(mid, [[0]], [s0], rows)
    s1, ahead, *rest = hold(s1, ahead, *q0, *mid)
    q0, mid = rest[:2], rest[2:]

    part_sums = step(mid, [1], [s1], ahead)
    j1 = joined(s1)
    part_sums, j1 = hold(part_sums, j1)
    q1 = (j1, swap(j1, "yh"))
    summed = z_sum(solve_part(half, rest_inverse, 1, rest_right, 1, [part_sums]))
    summed, *q1 = hold(summed, *q1)
    s2 = z_all(summed)
    ahead = update_part(mid, [[2, 3]], [s0, s1], rows)
    s2, ahead = hold(s2, ahead)

    part_sums = step(mid, [4], [s2], ahead)
    far = with_core(far)
    j2 = joined(s2)
    part_sums, j2, *far = hold(part_sums, j2, *far)
    summed = z_sum(solve_part(half, rest_inverse, 2, rest_right, 2, [part_sums]))
    before = update_part(far, [t[:3] for t in tails], [s0, s1, s2], rows)
    q2 = (j2, swap(j2, "yh"))
    summed, before, *q2 = hold(summed, before, *q2)
    s3 = z_all(summed)

    pieces = tail_part(yh1, far, [t[3:] for t in tails], s3, before, rows, nx)
    j3 = joined(s3)
    q3 = (j3, swap(j3, "yh"))
    own = lax.all_to_all(pieces, ("yh", "x"), 0, 0)
    out = place(yh1, core1, None, 0, [q0, q1, q2], shape)
    own, out = hold(own, out)
    final = lax.all_to_all(sum_groups(own, 2), "x", 0, 0)
    out = place(yh1, core1, out, 3, [q3], shape)
    final, out = hold(final, out)
    return out, finish(core1, [final, swap(final, "core")], right_side, chain)


def solution(mesh):
    fine = Mesh(mesh.devices.reshape(SIZES), AXES)
    return jax.shard_map(
        on_device,
        mesh=fine,
        in_specs=(
            P(None, ("yh", "z"), None, ("x", "core")),
            P(None, ("x", "core", "yl"), ("yh", "z")),
            P(None, ("yh", "z"), "yl"),
        ),
        out_specs=(P(None, ("x", "core"), "yl"), P(None, ("yh", "z"), "yl")),
        check_vma=False,
    )
```
